128 devices in a mesh: row: 8 (over y, core), col: 16 (over z, x).
Axes of the slice: x: 4, y: 4, z: 4, core: 2. Of those that a mesh axis runs over, the one named last changes fastest.
Arguments:
- features: float32 [256, 1024, 128], P('row', 'col'), may hold values from -0.4 to 0.4
- step_size: float32 [256, 1024, 128], P('row', 'col'), may hold values from 0.5 to 2
- write_weights: float32 [256, 1024, 16], P('row', 'col'), may hold values from -6 to 6
- read_weights: float32 [256, 1024, 16], P('row', 'col'), may hold values from -6 to 6
- decay_log: float32 [16, 128], replicated, may hold values from -7.6 to -3.5
- out_grad: float32 [256, 1024, 128], P('row', 'col'), may hold values from -0.4 to 0.4
Outputs:
- grad_features: float32 [256, 1024, 128], P('row', 'col')
- grad_step: float32 [256, 1024, 128], P('row', 'col')
- grad_write: float32 [256, 1024, 16], P('row', 'col')
- grad_read: float32 [256, 1024, 16], P('row', 'col')
- grad_decay: float32 [16, 128], replicated
The draws below stay inside these ranges and needn't reach their ends.
All inputs are finite; a program needn't handle non-finite values.
Results may differ from the reference program's by a relative error of at most 0.0002.
Values sent between devices are 32-bit elements; how exact they have to be, the bound alone decides.
A program may use at most 320 MiB of HBM per device.

```python
import math
import jax
import jax.numpy as jnp
from jax import lax

D = 128
NS = 16
H = 256
W = 1024


def shard_levels(stream_key, extent, split, low, largest):
    def one(axis_at, blocks):
        steps = jax.random.uniform(jax.random.fold_in(jax.random.fold_in(stream_key, 6), axis_at), (blocks,), jnp.float32, low / len(split), largest / len(split))
        return jnp.repeat(jnp.exp(steps), extent[axis_at] // blocks).reshape((-1,) + (1,) * (len(extent) - axis_at - 1))

    loudness = one(*split[0])
    for cut in split[1:]:
        loudness = loudness * one(*cut)
    return loudness


def gaussian(rng, dims, spread, bound, cuts=(), kind=jnp.bfloat16):
    result = spread * jax.random.normal(rng, dims, jnp.float32)
    if cuts:
        result = result * shard_levels(rng, dims, cuts, -0.22, 0.18)
    return jnp.clip(result, -bound, bound).astype(kind)


def setup_inputs(seed: int = 0) -> dict:
    keys = jax.random.split(jax.random.key(seed), 7)
    features = gaussian(keys[0], (H, W, D), 0.05, 0.4, ((0, 8), (1, 16)), jnp.float32)
    step_size = jnp.clip(jnp.exp(math.log(2.0) - 1.3862944 * jax.random.uniform(keys[1], (H, W, D), jnp.float32) ** shard_levels(keys[1], (H, W, D), ((0, 8), (1, 16)), -0.2, 0.2)), 0.5, 2.0)
    write_weights = gaussian(keys[2], (H, W, NS), 1.0, 6.0, ((0, 8), (1, 16)), jnp.float32)
    read_weights = gaussian(keys[3], (H, W, NS), 1.0, 6.0, ((0, 8), (1, 16)), jnp.float32)
    decay_log = jnp.clip(jax.random.uniform(keys[4], (NS, D), jnp.float32, -7.6, -3.5), -7.6, -3.5)
    out_grad = gaussian(keys[5], (H, W, D), 0.05, 0.4, ((0, 8), (1, 16)), jnp.float32)
    return {"features": features, "step_size": step_size, "write_weights": write_weights, "read_weights": read_weights, "decay_log": decay_log, "out_grad": out_grad}


def run_forward(decays, driving):
    def advance(current, inputs):
        factor, source = inputs
        current = factor * current + source
        return current, current
    _, states = lax.scan(advance, jnp.zeros(decays.shape[1:], jnp.float32), (decays, driving))
    return states


def run_backward(decays, driving):
    def retreat(passed, inputs):
        factor, source = inputs
        adjoint = source + passed
        return factor * adjoint, adjoint
    _, adjoints = lax.scan(retreat, jnp.zeros(decays.shape[1:], jnp.float32), (decays, driving), reverse=True)
    return adjoints


def transpose_grid(array):
    return jnp.swapaxes(array, 0, 1)


def reference(features, step_size, write_weights, read_weights, decay_log, out_grad):
    decay_rate = -jnp.exp(decay_log)
    write_by_state = jnp.moveaxis(write_weights, 2, 0)
    read_by_state = jnp.moveaxis(read_weights, 2, 0)
    source_base = step_size * features

    def one_state(carried, inputs):
        through, rate_term = carried
        rate_row, write_plane, read_plane = inputs
        decays = jnp.exp(step_size * rate_row[None, None, :])
        driving = source_base * write_plane[:, :, None]
        vertical = run_forward(decays, driving)
        states = transpose_grid(run_forward(transpose_grid(decays), transpose_grid(vertical)))
        direct = read_plane[:, :, None] * out_grad
        adjoint_h = transpose_grid(run_backward(transpose_grid(decays), transpose_grid(direct)))
        adjoint_v = run_backward(decays, adjoint_h)
        states_prev = jnp.concatenate([jnp.zeros_like(states[:, :1]), states[:, :-1]], 1)
        vert_prev = jnp.concatenate([jnp.zeros_like(vertical[:1]), vertical[:-1]], 0)
        exponent_grad = (adjoint_h * states_prev + adjoint_v * vert_prev) * decays
        through = through + adjoint_v * write_plane[:, :, None]
        rate_term = rate_term + exponent_grad * rate_row[None, None, :]
        write_col = jnp.sum(adjoint_v * source_base, axis=2)
        read_col = jnp.sum(states * out_grad, axis=2)
        decay_row = jnp.sum(exponent_grad * step_size, axis=(0, 1)) * rate_row
        return (through, rate_term), (write_col, read_col, decay_row)

    start = (jnp.zeros(features.shape, jnp.float32), jnp.zeros(features.shape, jnp.float32))
    (through, rate_term), (write_cols, read_cols, grad_decay) = lax.scan(
        one_state, start, (decay_rate, write_by_state, read_by_state))
    grad_features = step_size * through
    grad_step = features * through + rate_term
    grad_write = jnp.moveaxis(write_cols, 0, 2)
    grad_read = jnp.moveaxis(read_cols, 0, 2)
    return grad_features, grad_step, grad_write, grad_read, grad_decay
```

```python
import functools
import math
import jax
import jax.numpy as jnp
from jax import lax
from jax.experimental import pallas as pl
from jax.experimental.pallas import tpu as pltpu
from jax.sharding import PartitionSpec as P

NS = 16
D = 128
S = 8
F32 = jnp.float32
LOG2E = math.log2(math.e)
LN2 = math.log(2.0)
MESH = pl.DeviceIdType.MESH
VMEM = pl.BlockSpec(memory_space=pltpu.VMEM)


def column(ref, h, k, width):
    return ref[h, pl.ds(k, S, stride=width), :]


def spread(block, n):
    return jnp.broadcast_to(block[:, n : n + 1], (S, D))


def set_rates(decay_log, rates):
    for n in range(NS):
        rates[n] = jnp.broadcast_to(-jnp.exp(decay_log[n : n + 1, :]) * LOG2E, (S, D))


def sublane():
    return lax.broadcasted_iota(jnp.int32, (S, D), 0)


def sums_down(value, at):
    for shift in (1, 2, 4):
        value = value + jnp.where(at >= shift, pltpu.roll(value, shift, 0), 0.0)
    return value


def sums_up(value, at):
    for shift in (1, 2, 4):
        value = value + jnp.where(at < S - shift, pltpu.roll(value, S - shift, 0), 0.0)
    return value


def first_kernel(feat, step, write, read, grad, decay_log,
                 leave_v, sum_rows, leave_a, sum_cols, before, later, rates):
    rows, cols = step.shape[0], step.shape[1]
    K = cols // S
    set_rates(decay_log, rates)
    leave_v[...] = jnp.zeros_like(leave_v)
    sum_rows[...] = jnp.zeros_like(sum_rows)
    at = sublane()

    def row(h, carry):
        a = [jnp.zeros((S, D), F32)] * NS
        total = jnp.zeros((S, D), F32)
        for k in reversed(range(K)):
            dt = column(step, h, k, K)
            u = dt * column(feat, h, k, K)
            og = column(grad, h, k, K)
            wb = column(write, h, k, K)
            rb = column(read, h, k, K)
            total = total + dt
            sum_rows[k] += dt
            for n in range(NS):
                e = jnp.exp2(dt * rates[n])
                leave_v[k, n] = e * leave_v[k, n] + u * spread(wb, n)
                a[n] = e * (a[n] + spread(rb, n) * og)
        upto = sums_down(total, at)
        ahead = upto - total
        before[h] = ahead
        sum_cols[h] = upto[S - 1 :, :]
        for n in range(NS):
            m = jnp.exp2(rates[n] * ahead) * a[n]
            z = sums_up(m, at)
            leave_a[h, n : n + 1, :] = z[0:1, :]
            later[h, n] = z - m
        return carry

    lax.fori_loop(0, rows, row, 0)


def second_kernel(feat, step, write, read, grad, decay_log, from_above, from_right,
                  sum_cols, before, later, leave_s, earlier, leave_p, rates, vert):
    rows, cols = step.shape[0], step.shape[1]
    K = cols // S
    set_rates(decay_log, rates)
    vert[...] = from_above[...]
    leave_p[...] = jnp.zeros_like(leave_p)
    at = sublane()
    slow = -jnp.exp(decay_log[...]) * LOG2E

    def forward(h, carry):
        l = [jnp.zeros((S, D), F32)] * NS
        total = jnp.zeros((S, D), F32)
        for k in range(K):
            dt = column(step, h, k, K)
            u = dt * column(feat, h, k, K)
            wb = column(write, h, k, K)
            total = total + dt
            for n in range(NS):
                e = jnp.exp2(dt * rates[n])
                v = e * vert[k, n] + u * spread(wb, n)
                vert[k, n] = v
                l[n] = e * l[n] + v
        upto = before[h] + total
        whole = jnp.exp2(slow * sum_cols[h])
        for n in range(NS):
            m = jnp.exp2(-rates[n] * upto) * l[n]
            z = sums_down(m, at)
            leave_s[h, n : n + 1, :] = whole[n : n + 1, :] * z[S - 1 :, :]
            earlier[h, n] = z - m
        return carry

    def backward(i, carry):
        h = rows - 1 - i
        total = jnp.zeros((S, D), F32)
        for k in range(K):
            total = total + column(step, h, k, K)
        upto = before[h] + total
        entering = jnp.exp2(slow * sum_cols[h]) * from_right[h]
        a = [
            jnp.exp2(-rates[n] * upto) * (later[h, n] + entering[n : n + 1, :])
            for n in range(NS)
        ]
        for k in reversed(range(K)):
            dt = column(step, h, k, K)
            og = column(grad, h, k, K)
            rb = column(read, h, k, K)
            for n in range(NS):
                e = jnp.exp2(dt * rates[n])
                ah = a[n] + spread(rb, n) * og
                leave_p[k, n] = e * (ah + leave_p[k, n])
                a[n] = e * ah
        return carry

    lax.fori_loop(0, rows, forward, 0)
    lax.fori_loop(0, rows, backward, 0)


def third_kernel(feat, step, write, read, grad, decay_log, from_above, from_right, from_left,
                 from_below, sum_cols, before, later, earlier,
                 g_feat, g_step, g_write, g_read, g_decay, rates, vert, below, kept_s, kept_v):
    rows, cols = step.shape[0], step.shape[1]
    K = cols // S
    set_rates(decay_log, rates)
    vert[...] = from_above[...]
    below[...] = from_below[...]
    g_decay[...] = jnp.zeros_like(g_decay)
    lane = lax.broadcasted_iota(jnp.int32, (S, D), 1)
    slow = -jnp.exp(decay_log[...]) * LOG2E

    def forward(h, carry):
        ahead = before[h]
        s = [
            jnp.exp2(rates[n] * ahead) * (earlier[h, n] + from_left[h, n : n + 1, :])
            for n in range(NS)
        ]
        for k in range(K):
            dt = column(step, h, k, K)
            u = dt * column(feat, h, k, K)
            og = column(grad, h, k, K)
            wb = column(write, h, k, K)
            out = jnp.zeros((S, D), F32)
            for n in range(NS):
                e = jnp.exp2(dt * rates[n])
                q = e * vert[k, n]
                v = q + u * spread(wb, n)
                vert[k, n] = v
                t = e * s[n]
                s[n] = t + v
                kept_v[h, k, n] = q
                kept_s[h, k, n] = t
                out = jnp.where(lane == n, jnp.sum(s[n] * og, axis=1, keepdims=True), out)
            g_read[h, k] = out[:, :NS]
        return carry

    def backward(i, carry):
        h = rows - 1 - i
        total = jnp.zeros((S, D), F32)
        for k in range(K):
            total = total + column(step, h, k, K)
        upto = before[h] + total
        entering = jnp.exp2(slow * sum_cols[h]) * from_right[h]
        a = [
            jnp.exp2(-rates[n] * upto) * (later[h, n] + entering[n : n + 1, :])
            for n in range(NS)
        ]
        for k in reversed(range(K)):
            dt = column(step, h, k, K)
            fx = column(feat, h, k, K)
            u = dt * fx
            og = column(grad, h, k, K)
            wb = column(write, h, k, K)
            rb = column(read, h, k, K)
            out = jnp.zeros((S, D), F32)
            through = jnp.zeros((S, D), F32)
            rated = jnp.zeros((S, D), F32)
            for n in range(NS):
                e = jnp.exp2(dt * rates[n])
                ah = a[n] + spread(rb, n) * og
                av = ah + below[k, n]
                below[k, n] = e * av
                a[n] = e * ah
                eg = ah * kept_s[h, k, n] + av * kept_v[h, k, n]
                through = through + av * spread(wb, n)
                rated = rated + eg * rates[n]
                g_decay[n] += eg * dt
                out = jnp.where(lane == n, jnp.sum(av * u, axis=1, keepdims=True), out)
            g_write[h, k] = out[:, :NS]
            g_feat[h, pl.ds(k, S, stride=K), :] = dt * through
            g_step[h, pl.ds(k, S, stride=K), :] = fx * through + LN2 * rated
        return carry

    lax.fori_loop(0, rows, forward, 0)
    lax.fori_loop(0, rows, backward, 0)


def exchange_kernel(forward_rows, first, nr, nc, *refs):
    if first:
        (leave_r, sum_r, leave_c, sum_c, decay_log, got_r, got_c, sums_r, sums_c,
         in_r, in_c, out_r, out_c, s_out, s_in, b_out, b_in, q_out, q_in) = refs
    else:
        (leave_r, sums_r, leave_c, sums_c, decay_log, got_r, got_c,
         in_r, in_c, out_r, out_c, s_out, s_in, b_out, b_in) = refs
    ri, ci = lax.axis_index("row"), lax.axis_index("col")
    kr = leave_r.shape[0] // nr
    hc = leave_c.shape[0] // nc
    barrier = pltpu.get_barrier_semaphore()
    row_peers = [(lax.rem(ri + o, nr), ci) for o in range(1, nr)]
    col_peers = [(ri, lax.rem(ci + o, nc)) for o in range(1, nc)]
    for peer in row_peers + col_peers:
        pl.semaphore_signal(barrier, inc=1, device_id=peer, device_id_type=MESH)
    pl.semaphore_wait(barrier, len(row_peers) + len(col_peers))

    def send(src, dst, out_sem, in_sem, at, peer):
        copy = pltpu.make_async_remote_copy(
            src_ref=src, dst_ref=dst, send_sem=out_sem.at[at], recv_sem=in_sem.at[at],
            device_id=peer, device_id_type=MESH)
        copy.start()
        return copy

    copies = []
    for o, peer in enumerate(row_peers):
        src = leave_r.at[pl.ds(peer[0] * kr, kr)]
        copies.append(send(src, in_r.at[ri], s_out, s_in, o, peer))
        if first:
            src = sum_r.at[pl.ds(peer[0] * kr, kr)]
            copies.append(send(src, sums_r.at[ri], q_out, q_in, o, peer))
    for o, peer in enumerate(col_peers):
        src = leave_c.at[pl.ds(peer[1] * hc, hc)]
        copies.append(send(src, in_c.at[ci], s_out, s_in, nr - 1 + o, peer))
        if first:
            src = sum_c.at[pl.ds(peer[1] * hc, hc)]
            copies.append(send(src, sums_c.at[ci], q_out, q_in, nr - 1 + o, peer))
    in_r[ri] = leave_r[pl.ds(ri * kr, kr)]
    in_c[ci] = leave_c[pl.ds(ci * hc, hc)]
    if first:
        sums_r[ri] = sum_r[pl.ds(ri * kr, kr)]
        sums_c[ci] = sum_c[pl.ds(ci * hc, hc)]
    for copy in copies:
        copy.wait()
    rate = -jnp.exp(decay_log[...]) * LOG2E

    for j in range(hc):
        now = jnp.zeros((NS, D), F32)
        for c in (reversed(range(nc)) if forward_rows else range(nc)):
            out_c[c, j] = now
            now = jnp.exp2(rate * sums_c[c, j]) * now + in_c[c, j]

    def scan_row(i, carry):
        for j in range(kr):
            r2 = -jnp.exp(decay_log[pl.ds(i, 1), :]) * LOG2E
            now = jnp.zeros((S, D), F32)
            for r in (range(nr) if forward_rows else reversed(range(nr))):
                out_r[r, j, i] = now
                now = jnp.exp2(r2 * sums_r[r, j]) * now + in_r[r, j, i]
        return carry

    back = []
    for o, peer in enumerate(col_peers):
        back.append(send(out_c.at[peer[1]], got_c.at[pl.ds(ci * hc, hc)], b_out, b_in,
                         nr - 1 + o, peer))
    lax.fori_loop(0, NS, scan_row, 0)
    for o, peer in enumerate(row_peers):
        back.append(send(out_r.at[peer[0]], got_r.at[pl.ds(ri * kr, kr)], b_out, b_in, o, peer))
    got_c[pl.ds(ci * hc, hc)] = out_c[ci]
    got_r[pl.ds(ri * kr, kr)] = out_r[ri]
    for copy in back:
        copy.wait()


def exchange(forward_rows, first, nr, nc, leave_r, sum_r, leave_c, sum_c, decay_log):
    K, rows = leave_r.shape[0], leave_c.shape[0]
    kr, hc = K // nr, rows // nc
    peers = nr + nc - 2
    sds = jax.ShapeDtypeStruct
    outs = [sds(leave_r.shape, F32), sds(leave_c.shape, F32)]
    if first:
        outs += [sds((nr, kr, S, D), F32), sds((nc, hc, 1, D), F32)]
    dma = pltpu.SemaphoreType.DMA((peers,))
    return pl.pallas_call(
        functools.partial(exchange_kernel, forward_rows, first, nr, nc),
        out_shape=outs,
        in_specs=[VMEM] * 5,
        out_specs=[VMEM] * len(outs),
        scratch_shapes=[
            pltpu.VMEM((nr, kr, NS, S, D), F32),
            pltpu.VMEM((nc, hc, NS, D), F32),
            pltpu.VMEM((nr, kr, NS, S, D), F32),
            pltpu.VMEM((nc, hc, NS, D), F32),
        ] + [dma] * (6 if first else 4),
        compiler_params=pltpu.CompilerParams(
            collective_id=0 if first else 1, has_side_effects=True,
            vmem_limit_bytes=16 << 20),
        name="exchange_first" if first else "exchange_second",
    )(leave_r, sum_r, leave_c, sum_c, decay_log)


def shards(features, step_size, write_weights, read_weights, decay_log, out_grad):
    rows, cols = step_size.shape[0], step_size.shape[1]
    K = cols // S
    nr, nc = lax.axis_size("row"), lax.axis_size("col")
    sds = jax.ShapeDtypeStruct
    raw = (features, step_size, write_weights, read_weights, out_grad, decay_log)
    carry_r, carry_c = (K, NS, S, D), (rows, NS, D)
    rates = pltpu.VMEM((NS, S, D), F32)

    def call(kernel, outs, scratch, args, limit):
        return pl.pallas_call(
            kernel,
            out_shape=[sds(o, F32) for o in outs],
            in_specs=[VMEM] * len(args),
            out_specs=[VMEM] * len(outs),
            scratch_shapes=scratch,
            compiler_params=pltpu.CompilerParams(vmem_limit_bytes=limit << 20),
        )(*args)

    leave_v, sum_rows, leave_a, sum_cols, before, later = call(
        first_kernel,
        [carry_r, (K, S, D), carry_c, (rows, 1, D), (rows, S, D), (rows, NS, S, D)],
        [rates], raw, 24)
    from_above, from_right, sums_r, sums_c = exchange(
        True, True, nr, nc, leave_v, sum_rows, leave_a, sum_cols, decay_log)
    leave_s, earlier, leave_p = call(
        second_kernel,
        [carry_c, (rows, NS, S, D), carry_r],
        [rates, pltpu.VMEM(carry_r, F32)],
        raw + (from_above, from_right, sum_cols, before, later), 24)
    from_below, from_left = exchange(
        False, False, nr, nc, leave_p, sums_r, leave_s, sums_c, decay_log)
    g_feat, g_step, g_write, g_read, g_decay = call(
        third_kernel,
        [(rows, cols, D), (rows, cols, D), (rows, K, S, NS), (rows, K, S, NS), (NS, S, D)],
        [rates, pltpu.VMEM(carry_r, F32), pltpu.VMEM(carry_r, F32),
         pltpu.VMEM((rows, K, NS, S, D), F32), pltpu.VMEM((rows, K, NS, S, D), F32)],
        raw + (from_above, from_right, from_left, from_below, sum_cols, before, later, earlier),
        58)

    def as_columns(g):
        return g.transpose(0, 2, 1, 3).reshape(rows, cols, NS)

    rate = -jnp.exp(decay_log)
    g_decay = lax.psum(jnp.sum(g_decay, axis=1), ("row", "col")) * rate
    return (g_feat, g_step, as_columns(g_write), as_columns(g_read), g_decay)


def solution(mesh):
    tiles = P("row", "col", None)
    in_specs = (tiles, tiles, tiles, tiles, P(), tiles)
    out_specs = (tiles, tiles, tiles, tiles, P())
    return jax.shard_map(shards, mesh=mesh, in_specs=in_specs, out_specs=out_specs, check_vma=False)
```

```python
import functools
import math
import jax
import jax.numpy as jnp
from jax import lax
from jax.experimental import pallas as pl
from jax.experimental.pallas import tpu as pltpu
from jax.sharding import PartitionSpec as P

NS = 16
D = 128
S = 8
F32 = jnp.float32
LOG2E = math.log2(math.e)
LN2 = math.log(2.0)
MESH = pl.DeviceIdType.MESH
VMEM = pl.BlockSpec(memory_space=pltpu.VMEM)


def column(ref, h, k, width):
    return ref[h, pl.ds(k, S, stride=width), :]


def spread(block, n):
    return jnp.broadcast_to(block[:, n : n + 1], (S, D))


def set_rates(decay_log, rates):
    for n in range(NS):
        rates[n] = jnp.broadcast_to(-jnp.exp(decay_log[n : n + 1, :]) * LOG2E, (S, D))


def sublane():
    return lax.broadcasted_iota(jnp.int32, (S, D), 0)


def sums_down(value, at):
    for shift in (1, 2, 4):
        value = value + jnp.where(at >= shift, pltpu.roll(value, shift, 0), 0.0)
    return value


def sums_up(value, at):
    for shift in (1, 2, 4):
        value = value + jnp.where(at < S - shift, pltpu.roll(value, S - shift, 0), 0.0)
    return value


def set_selector(selector):
    of = lax.broadcasted_iota(jnp.int32, selector.shape, 0) // D
    to = lax.broadcasted_iota(jnp.int32, selector.shape, 1)
    selector[...] = jnp.where(of == to, 1.0, 0.0).astype(jnp.bfloat16)


def channel_sums(products, selector):
    values = products[...]
    high = values.astype(jnp.bfloat16)
    low = (values - high.astype(F32)).astype(jnp.bfloat16)
    both = jnp.concatenate([high, low], axis=0)
    sums = jnp.dot(both, selector[...], preferred_element_type=F32)
    size = values.shape[0]
    return (sums[:size] + sums[size:])[:, :NS]


def first_kernel(feat, step, write, read, grad, decay_log,
                 leave_v, sum_rows, leave_a, sum_cols, before, later, rates):
    rows, cols = step.shape[0], step.shape[1]
    K = cols // S
    set_rates(decay_log, rates)
    leave_v[...] = jnp.zeros_like(leave_v)
    sum_rows[...] = jnp.zeros_like(sum_rows)
    at = sublane()

    def row(h, carry):
        a = [jnp.zeros((S, D), F32)] * NS
        total = jnp.zeros((S, D), F32)
        for k in reversed(range(K)):
            dt = column(step, h, k, K)
            u = dt * column(feat, h, k, K)
            og = column(grad, h, k, K)
            wb = column(write, h, k, K)
            rb = column(read, h, k, K)
            total = total + dt
            sum_rows[k] += dt
            for n in range(NS):
                e = jnp.exp2(dt * rates[n])
                leave_v[k, n] = e * leave_v[k, n] + u * spread(wb, n)
                a[n] = e * (a[n] + spread(rb, n) * og)
        upto = sums_down(total, at)
        ahead = upto - total
        before[h] = ahead
        sum_cols[h] = upto[S - 1 :, :]
        for n in range(NS):
            m = jnp.exp2(rates[n] * ahead) * a[n]
            z = sums_up(m, at)
            leave_a[h, n : n + 1, :] = z[0:1, :]
            later[h, n] = z - m
        return carry

    lax.fori_loop(0, rows, row, 0)


def second_kernel(feat, step, write, read, grad, decay_log, from_above, from_right,
                  sum_cols, before, later, leave_s, earlier, leave_p, rates, vert):
    rows, cols = step.shape[0], step.shape[1]
    K = cols // S
    set_rates(decay_log, rates)
    vert[...] = from_above[...]
    leave_p[...] = jnp.zeros_like(leave_p)
    at = sublane()
    slow = -jnp.exp(decay_log[...]) * LOG2E

    def forward(h, carry):
        l = [jnp.zeros((S, D), F32)] * NS
        total = jnp.zeros((S, D), F32)
        for k in range(K):
            dt = column(step, h, k, K)
            u = dt * column(feat, h, k, K)
            wb = column(write, h, k, K)
            total = total + dt
            for n in range(NS):
                e = jnp.exp2(dt * rates[n])
                v = e * vert[k, n] + u * spread(wb, n)
                vert[k, n] = v
                l[n] = e * l[n] + v
        upto = before[h] + total
        whole = jnp.exp2(slow * sum_cols[h])
        for n in range(NS):
            m = jnp.exp2(-rates[n] * upto) * l[n]
            z = sums_down(m, at)
            leave_s[h, n : n + 1, :] = whole[n : n + 1, :] * z[S - 1 :, :]
            earlier[h, n] = z - m
        return carry

    def backward(i, carry):
        h = rows - 1 - i
        total = jnp.zeros((S, D), F32)
        for k in range(K):
            total = total + column(step, h, k, K)
        upto = before[h] + total
        entering = jnp.exp2(slow * sum_cols[h]) * from_right[h]
        a = [
            jnp.exp2(-rates[n] * upto) * (later[h, n] + entering[n : n + 1, :])
            for n in range(NS)
        ]
        for k in reversed(range(K)):
            dt = column(step, h, k, K)
            og = column(grad, h, k, K)
            rb = column(read, h, k, K)
            for n in range(NS):
                e = jnp.exp2(dt * rates[n])
                ah = a[n] + spread(rb, n) * og
                leave_p[k, n] = e * (ah + leave_p[k, n])
                a[n] = e * ah
        return carry

    lax.fori_loop(0, rows, forward, 0)
    lax.fori_loop(0, rows, backward, 0)


def third_kernel(feat, step, write, read, grad, decay_log, from_above, from_right, from_left,
                 from_below, sum_cols, before, later, earlier,
                 g_feat, g_step, g_write, g_read, g_decay, rates, vert, below, kept_s, kept_v, products, selector):
    rows, cols = step.shape[0], step.shape[1]
    K = cols // S
    set_rates(decay_log, rates)
    vert[...] = from_above[...]
    below[...] = from_below[...]
    g_decay[...] = jnp.zeros_like(g_decay)
    set_selector(selector)
    slow = -jnp.exp(decay_log[...]) * LOG2E

    def forward(h, carry):
        ahead = before[h]
        s = [
            jnp.exp2(rates[n] * ahead) * (earlier[h, n] + from_left[h, n : n + 1, :])
            for n in range(NS)
        ]
        for k in range(K):
            dt = column(step, h, k, K)
            u = dt * column(feat, h, k, K)
            og = column(grad, h, k, K)
            wb = column(write, h, k, K)
            for n in range(NS):
                e = jnp.exp2(dt * rates[n])
                q = e * vert[k, n]
                v = q + u * spread(wb, n)
                vert[k, n] = v
                t = e * s[n]
                s[n] = t + v
                kept_v[h, k, n] = q
                kept_s[h, k, n] = t
                products[S * k : S * k + S, D * n : D * n + D] = s[n] * og
        g_read[h] = channel_sums(products, selector)
        return carry

    def backward(i, carry):
        h = rows - 1 - i
        total = jnp.zeros((S, D), F32)
        for k in range(K):
            total = total + column(step, h, k, K)
        upto = before[h] + total
        entering = jnp.exp2(slow * sum_cols[h]) * from_right[h]
        a = [
            jnp.exp2(-rates[n] * upto) * (later[h, n] + entering[n : n + 1, :])
            for n in range(NS)
        ]
        for k in reversed(range(K)):
            dt = column(step, h, k, K)
            fx = column(feat, h, k, K)
            u = dt * fx
            og = column(grad, h, k, K)
            wb = column(write, h, k, K)
            rb = column(read, h, k, K)
            through = jnp.zeros((S, D), F32)
            rated = jnp.zeros((S, D), F32)
            for n in range(NS):
                e = jnp.exp2(dt * rates[n])
                ah = a[n] + spread(rb, n) * og
                av = ah + below[k, n]
                below[k, n] = e * av
                a[n] = e * ah
                eg = ah * kept_s[h, k, n] + av * kept_v[h, k, n]
                through = through + av * spread(wb, n)
                rated = rated + eg * rates[n]
                g_decay[n] += eg * dt
                products[S * k : S * k + S, D * n : D * n + D] = av * u
            g_feat[h, pl.ds(k, S, stride=K), :] = dt * through
            g_step[h, pl.ds(k, S, stride=K), :] = fx * through + LN2 * rated
        g_write[h] = channel_sums(products, selector)
        return carry

    lax.fori_loop(0, rows, forward, 0)
    lax.fori_loop(0, rows, backward, 0)


def exchange_kernel(forward_rows, first, nr, nc, *refs):
    if first:
        (leave_r, sum_r, leave_c, sum_c, decay_log, got_r, got_c, sums_r, sums_c,
         in_r, in_c, out_r, out_c, s_out, s_in, b_out, b_in, q_out, q_in) = refs
    else:
        (leave_r, sums_r, leave_c, sums_c, decay_log, got_r, got_c,
         in_r, in_c, out_r, out_c, s_out, s_in, b_out, b_in) = refs
    ri, ci = lax.axis_index("row"), lax.axis_index("col")
    kr = leave_r.shape[0] // nr
    hc = leave_c.shape[0] // nc
    barrier = pltpu.get_barrier_semaphore()
    row_peers = [(lax.rem(ri + o, nr), ci) for o in range(1, nr)]
    col_peers = [(ri, lax.rem(ci + o, nc)) for o in range(1, nc)]
    for peer in row_peers + col_peers:
        pl.semaphore_signal(barrier, inc=1, device_id=peer, device_id_type=MESH)
    pl.semaphore_wait(barrier, len(row_peers) + len(col_peers))

    def send(src, dst, out_sem, in_sem, at, peer):
        copy = pltpu.make_async_remote_copy(
            src_ref=src, dst_ref=dst, send_sem=out_sem.at[at], recv_sem=in_sem.at[at],
            device_id=peer, device_id_type=MESH)
        copy.start()
        return copy

    copies = []
    for o, peer in enumerate(row_peers):
        src = leave_r.at[pl.ds(peer[0] * kr, kr)]
        copies.append(send(src, in_r.at[ri], s_out, s_in, o, peer))
        if first:
            src = sum_r.at[pl.ds(peer[0] * kr, kr)]
            copies.append(send(src, sums_r.at[ri], q_out, q_in, o, peer))
    for o, peer in enumerate(col_peers):
        src = leave_c.at[pl.ds(peer[1] * hc, hc)]
        copies.append(send(src, in_c.at[ci], s_out, s_in, nr - 1 + o, peer))
        if first:
            src = sum_c.at[pl.ds(peer[1] * hc, hc)]
            copies.append(send(src, sums_c.at[ci], q_out, q_in, nr - 1 + o, peer))
    in_r[ri] = leave_r[pl.ds(ri * kr, kr)]
    in_c[ci] = leave_c[pl.ds(ci * hc, hc)]
    if first:
        sums_r[ri] = sum_r[pl.ds(ri * kr, kr)]
        sums_c[ci] = sum_c[pl.ds(ci * hc, hc)]
    for copy in copies:
        copy.wait()
    rate = -jnp.exp(decay_log[...]) * LOG2E

    for j in range(hc):
        now = jnp.zeros((NS, D), F32)
        for c in (reversed(range(nc)) if forward_rows else range(nc)):
            out_c[c, j] = now
            now = jnp.exp2(rate * sums_c[c, j]) * now + in_c[c, j]

    def scan_row(i, carry):
        for j in range(kr):
            r2 = -jnp.exp(decay_log[pl.ds(i, 1), :]) * LOG2E
            now = jnp.zeros((S, D), F32)
            for r in (range(nr) if forward_rows else reversed(range(nr))):
                out_r[r, j, i] = now
                now = jnp.exp2(r2 * sums_r[r, j]) * now + in_r[r, j, i]
        return carry

    back = []
    for o, peer in enumerate(col_peers):
        back.append(send(out_c.at[peer[1]], got_c.at[pl.ds(ci * hc, hc)], b_out, b_in,
                         nr - 1 + o, peer))
    lax.fori_loop(0, NS, scan_row, 0)
    for o, peer in enumerate(row_peers):
        back.append(send(out_r.at[peer[0]], got_r.at[pl.ds(ri * kr, kr)], b_out, b_in, o, peer))
    got_c[pl.ds(ci * hc, hc)] = out_c[ci]
    got_r[pl.ds(ri * kr, kr)] = out_r[ri]
    for copy in back:
        copy.wait()


def exchange(forward_rows, first, nr, nc, leave_r, sum_r, leave_c, sum_c, decay_log):
    K, rows = leave_r.shape[0], leave_c.shape[0]
    kr, hc = K // nr, rows // nc
    peers = nr + nc - 2
    sds = jax.ShapeDtypeStruct
    outs = [sds(leave_r.shape, F32), sds(leave_c.shape, F32)]
    if first:
        outs += [sds((nr, kr, S, D), F32), sds((nc, hc, 1, D), F32)]
    dma = pltpu.SemaphoreType.DMA((peers,))
    return pl.pallas_call(
        functools.partial(exchange_kernel, forward_rows, first, nr, nc),
        out_shape=outs,
        in_specs=[VMEM] * 5,
        out_specs=[VMEM] * len(outs),
        scratch_shapes=[
            pltpu.VMEM((nr, kr, NS, S, D), F32),
            pltpu.VMEM((nc, hc, NS, D), F32),
            pltpu.VMEM((nr, kr, NS, S, D), F32),
            pltpu.VMEM((nc, hc, NS, D), F32),
        ] + [dma] * (6 if first else 4),
        compiler_params=pltpu.CompilerParams(
            collective_id=0 if first else 1, has_side_effects=True,
            vmem_limit_bytes=16 << 20),
        name="exchange_first" if first else "exchange_second",
    )(leave_r, sum_r, leave_c, sum_c, decay_log)


def total_kernel(nr, nc, part, decay_log, out, by_row, by_col, s_out, s_in):
    ri, ci = lax.axis_index("row"), lax.axis_index("col")
    row_peers = [(lax.rem(ri + o, nr), ci) for o in range(1, nr)]
    col_peers = [(ri, lax.rem(ci + o, nc)) for o in range(1, nc)]
    barrier = pltpu.get_barrier_semaphore()
    for peer in row_peers + col_peers:
        pl.semaphore_signal(barrier, inc=1, device_id=peer, device_id_type=MESH)
    pl.semaphore_wait(barrier, len(row_peers) + len(col_peers))

    def stage(value, box, mine, peers, base):
        box[mine] = value
        copies = []
        for o, peer in enumerate(peers):
            copy = pltpu.make_async_remote_copy(
                src_ref=box.at[mine], dst_ref=box.at[mine], send_sem=s_out.at[base + o],
                recv_sem=s_in.at[base + o], device_id=peer, device_id_type=MESH)
            copy.start()
            copies.append(copy)
        for copy in copies:
            copy.wait()
        return jnp.sum(box[...], axis=0)

    value = stage(jnp.sum(part[...], axis=1), by_row, ri, row_peers, 0)
    value = stage(value, by_col, ci, col_peers, nr - 1)
    out[...] = value * -jnp.exp(decay_log[...])


def total(nr, nc, part, decay_log):
    dma = pltpu.SemaphoreType.DMA((nr + nc - 2,))
    return pl.pallas_call(
        functools.partial(total_kernel, nr, nc),
        out_shape=jax.ShapeDtypeStruct((NS, D), F32),
        in_specs=[VMEM] * 2,
        out_specs=VMEM,
        scratch_shapes=[pltpu.VMEM((nr, NS, D), F32), pltpu.VMEM((nc, NS, D), F32), dma, dma],
        compiler_params=pltpu.CompilerParams(
            collective_id=2, has_side_effects=True, vmem_limit_bytes=4 << 20),
        name="total",
    )(part, decay_log)


def shards(features, step_size, write_weights, read_weights, decay_log, out_grad):
    rows, cols = step_size.shape[0], step_size.shape[1]
    K = cols // S
    nr, nc = lax.axis_size("row"), lax.axis_size("col")
    sds = jax.ShapeDtypeStruct
    raw = (features, step_size, write_weights, read_weights, out_grad, decay_log)
    carry_r, carry_c = (K, NS, S, D), (rows, NS, D)
    rates = pltpu.VMEM((NS, S, D), F32)

    def call(kernel, outs, scratch, args, limit):
        return pl.pallas_call(
            kernel,
            out_shape=[sds(o, F32) for o in outs],
            in_specs=[VMEM] * len(args),
            out_specs=[VMEM] * len(outs),
            scratch_shapes=scratch,
            compiler_params=pltpu.CompilerParams(vmem_limit_bytes=limit << 20),
        )(*args)

    leave_v, sum_rows, leave_a, sum_cols, before, later = call(
        first_kernel,
        [carry_r, (K, S, D), carry_c, (rows, 1, D), (rows, S, D), (rows, NS, S, D)],
        [rates], raw, 24)
    from_above, from_right, sums_r, sums_c = exchange(
        True, True, nr, nc, leave_v, sum_rows, leave_a, sum_cols, decay_log)
    leave_s, earlier, leave_p = call(
        second_kernel,
        [carry_c, (rows, NS, S, D), carry_r],
        [rates, pltpu.VMEM(carry_r, F32)],
        raw + (from_above, from_right, sum_cols, before, later), 24)
    from_below, from_left = exchange(
        False, False, nr, nc, leave_p, sums_r, leave_s, sums_c, decay_log)
    g_feat, g_step, g_write, g_read, g_decay = call(
        third_kernel,
        [(rows, cols, D), (rows, cols, D), (rows, cols, NS), (rows, cols, NS), (NS, S, D)],
        [rates, pltpu.VMEM(carry_r, F32), pltpu.VMEM(carry_r, F32),
         pltpu.VMEM((rows, K, NS, S, D), F32), pltpu.VMEM((rows, K, NS, S, D), F32),
         pltpu.VMEM((cols, NS * D), F32), pltpu.VMEM((NS * D, D), jnp.bfloat16)],
        raw + (from_above, from_right, from_left, from_below, sum_cols, before, later, earlier),
        58)

    def as_columns(g):
        return g.reshape(rows, K, S, NS).transpose(0, 2, 1, 3).reshape(rows, cols, NS)

    g_decay = total(nr, nc, g_decay, decay_log)
    return (g_feat, g_step, as_columns(g_write), as_columns(g_read), g_decay)


def solution(mesh):
    tiles = P("row", "col", None)
    in_specs = (tiles, tiles, tiles, tiles, P(), tiles)
    out_specs = (tiles, tiles, tiles, tiles, P())
    return jax.shard_map(shards, mesh=mesh, in_specs=in_specs, out_specs=out_specs, check_vma=False)
```

```python
import functools
import math
import jax
import jax.numpy as jnp
from jax import lax
from jax.experimental import pallas as pl
from jax.experimental.pallas import tpu as pltpu
from jax.sharding import PartitionSpec as P

NS = 16
HALF = 8
D = 128
S = 8
BLOCK = 4
F32 = jnp.float32
BF16 = jnp.bfloat16
LOG2E = math.log2(math.e)
LN2 = math.log(2.0)
MESH = pl.DeviceIdType.MESH
VMEM = pl.BlockSpec(memory_space=pltpu.VMEM)


def column(ref, h, k, width):
    return ref[h, pl.ds(k, S, stride=width), :]


def set_rates(decay_log, rates):
    for n in range(NS):
        rates[n] = jnp.broadcast_to(-jnp.exp(decay_log[n : n + 1, :]) * LOG2E, (S, D))


def equal(a, b):
    return jnp.where(a == b, 1.0, 0.0).astype(BF16)


def set_spreader(spreader):
    of = lax.broadcasted_iota(jnp.int32, spreader.shape, 0) % NS
    to = lax.broadcasted_iota(jnp.int32, spreader.shape, 1) // D
    spreader[...] = equal(of, to)


def set_selector(selector):
    of = lax.broadcasted_iota(jnp.int32, selector.shape, 0) // D
    to = lax.broadcasted_iota(jnp.int32, selector.shape, 1)
    selector[...] = equal(of, to)


def by_segment(cols):
    K = cols // S
    at = lax.broadcasted_iota(jnp.int32, (cols, cols), 0)
    col = lax.broadcasted_iota(jnp.int32, (cols, cols), 1)
    return equal(col, (at % S) * K + at // S)


def split3(x, axis):
    high = x.astype(BF16)
    rest = x - high.astype(F32)
    mid = rest.astype(BF16)
    low = (rest - mid.astype(F32)).astype(BF16)
    return jnp.concatenate([high, mid, low], axis=axis)


def spread(coded, spreader, pair):
    return jnp.dot(coded, spreader[:, 2 * D * pair : 2 * D * pair + 2 * D],
                   preferred_element_type=F32)


def sublane():
    return lax.broadcasted_iota(jnp.int32, (S, D), 0)


def sums_down(value, at):
    for shift in (1, 2, 4):
        value = value + jnp.where(at >= shift, pltpu.roll(value, shift, 0), 0.0)
    return value


def sums_up(value, at):
    for shift in (1, 2, 4):
        value = value + jnp.where(at < S - shift, pltpu.roll(value, S - shift, 0), 0.0)
    return value


def tile_of(block, row, half):
    return block[row : row + S, D * half : D * half + D]


def carries_kernel(nr, nc, feat, step, write, read, grad, decay_log,
                   from_above, from_right, from_left, from_below,
                   sum_cols, before, later, earlier, coded,
                   rates, spreader, drive, vert, leave_v, leave_a, leave_p, leave_s, sum_rows,
                   sums_r, sums_c, in_r, in_c, out_r, out_c,
                   s_out, s_in, b_out, b_in, q_out, q_in):
    rows, cols = step.shape[0], step.shape[1]
    K = cols // S
    ri, ci = lax.axis_index("row"), lax.axis_index("col")
    kr, hc = K // nr, rows // nc
    row_peers = [(lax.rem(ri + o, nr), ci) for o in range(1, nr)]
    col_peers = [(ri, lax.rem(ci + o, nc)) for o in range(1, nc)]
    barrier = pltpu.get_barrier_semaphore()
    for peer in row_peers + col_peers:
        pl.semaphore_signal(barrier, inc=1, device_id=peer, device_id_type=MESH)

    set_rates(decay_log, rates)
    set_spreader(spreader)
    slow = -jnp.exp(decay_log[...]) * LOG2E
    at = sublane()
    turn = by_segment(cols)

    def code(h, carry):
        for i, ref in enumerate((write, read)):
            parts = split3(ref[h], 0)
            coded[h, cols * i : cols * i + cols, :] = lax.dot_general(
                turn, parts, (((1,), (1,)), ((), ())), preferred_element_type=F32).astype(BF16)
        return carry

    lax.fori_loop(0, rows, code, 0, unroll=4)
    leave_v[...] = jnp.zeros_like(leave_v)
    leave_p[...] = jnp.zeros_like(leave_p)
    sum_rows[...] = jnp.zeros_like(sum_rows)

    def local_leaves(half):
        def row(h, carry):
            total = jnp.zeros((S, D), F32)
            for k in range(K):
                dt = column(step, h, k, K)
                drive[k] = dt * column(feat, h, k, K)
                if half == 0:
                    total = total + dt
                    sum_rows[k] += dt
            if half == 0:
                upto = sums_down(total, at)
                before[h] = upto - total
                sum_cols[h] = upto[S - 1 :, :]
            ahead = before[h]
            both = coded[h]
            for pair in range(HALF // 2):
                spreads = spread(both, spreader, half * HALF // 2 + pair)
                for j in range(2):
                    i = 2 * pair + j
                    n = half * HALF + i
                    a = jnp.zeros((S, D), F32)
                    r2 = rates[n]
                    for k in reversed(range(K)):
                        e = jnp.exp2(column(step, h, k, K) * r2)
                        leave_v[half, k, i] = (
                            e * leave_v[half, k, i] + drive[k] * tile_of(spreads, S * k, j))
                        a = e * (a + tile_of(spreads, cols + S * k, j) * column(grad, h, k, K))
                    m = jnp.exp2(r2 * ahead) * a
                    z = sums_up(m, at)
                    leave_a[half, h, i : i + 1, :] = z[0:1, :]
                    later[h, n] = z - m
            return carry

        lax.fori_loop(0, rows, row, 0)

    def carried_leaves(half):
        vert[half] = from_above[half]

        def row(step_at, carry):
            h = step_at
            b = rows - 1 - step_at
            total_h = jnp.zeros((S, D), F32)
            total_b = jnp.zeros((S, D), F32)
            for k in range(K):
                dt = column(step, h, k, K)
                drive[k] = dt * column(feat, h, k, K)
                total_h = total_h + dt
                total_b = total_b + column(step, b, k, K)
            upto_h = before[h] + total_h
            upto_b = before[b] + total_b
            rate = slow[half * HALF : half * HALF + HALF]
            whole = jnp.exp2(rate * sum_cols[h])
            entering = jnp.exp2(rate * sum_cols[b]) * from_right[half, b]
            both = jnp.concatenate([coded[h, :cols, :], coded[b, cols:, :]], axis=0)
            for pair in range(HALF // 2):
                spreads = spread(both, spreader, half * HALF // 2 + pair)
                for j in range(2):
                    i = 2 * pair + j
                    n = half * HALF + i
                    r2 = rates[n]
                    l = jnp.zeros((S, D), F32)
                    for k in range(K):
                        e = jnp.exp2(column(step, h, k, K) * r2)
                        v = e * vert[half, k, i] + drive[k] * tile_of(spreads, S * k, j)
                        vert[half, k, i] = v
                        l = e * l + v
                    m = jnp.exp2(-r2 * upto_h) * l
                    z = sums_down(m, at)
                    leave_s[half, h, i : i + 1, :] = whole[i : i + 1, :] * z[S - 1 :, :]
                    earlier[h, n] = z - m
                    a = jnp.exp2(-r2 * upto_b) * (later[b, n] + entering[i : i + 1, :])
                    for k in reversed(range(K)):
                        e = jnp.exp2(column(step, b, k, K) * r2)
                        ah = a + tile_of(spreads, cols + S * k, j) * column(grad, b, k, K)
                        leave_p[half, k, i] = e * (ah + leave_p[half, k, i])
                        a = e * ah
            return carry

        lax.fori_loop(0, rows, row, 0)

    def send(src, dst, out_sem, in_sem, peer):
        copy = pltpu.make_async_remote_copy(
            src_ref=src, dst_ref=dst, send_sem=out_sem, recv_sem=in_sem,
            device_id=peer, device_id_type=MESH)
        copy.start()
        return copy

    def scatter(x, half, leave_r, leave_c):
        copies = []
        for o, peer in enumerate(row_peers):
            copies.append(send(leave_r.at[half, pl.ds(peer[0] * kr, kr)], in_r.at[x, half, ri],
                               s_out.at[x, half, o], s_in.at[x, half, o], peer))
            if x == 0 and half == 0:
                copies.append(send(sum_rows.at[pl.ds(peer[0] * kr, kr)], sums_r.at[ri],
                                   q_out.at[o], q_in.at[o], peer))
        for p, peer in enumerate(col_peers):
            o = nr - 1 + p
            copies.append(send(leave_c.at[half, pl.ds(peer[1] * hc, hc)], in_c.at[x, half, ci],
                               s_out.at[x, half, o], s_in.at[x, half, o], peer))
            if x == 0 and half == 0:
                copies.append(send(sum_cols.at[pl.ds(peer[1] * hc, hc)], sums_c.at[ci],
                                   q_out.at[o], q_in.at[o], peer))
        in_r[x, half, ri] = leave_r[half, pl.ds(ri * kr, kr)]
        in_c[x, half, ci] = leave_c[half, pl.ds(ci * hc, hc)]
        if x == 0 and half == 0:
            sums_r[ri] = sum_rows[pl.ds(ri * kr, kr)]
            sums_c[ci] = sum_cols[pl.ds(ci * hc, hc)]
        return copies

    def give_back(x, half, waiting, got_r, got_c):
        for copy in waiting:
            copy.wait()
        rate = slow[half * HALF : half * HALF + HALF]
        for j in range(hc):
            now = jnp.zeros((HALF, D), F32)
            for c in (reversed(range(nc)) if x == 0 else range(nc)):
                out_c[x, half, c, j] = now
                now = jnp.exp2(rate * sums_c[c, j]) * now + in_c[x, half, c, j]

        def scan_row(i, carry):
            r2 = rates[half * HALF + i]
            for j in range(kr):
                now = jnp.zeros((S, D), F32)
                for r in (range(nr) if x == 0 else reversed(range(nr))):
                    out_r[x, half, r, j, i] = now
                    now = jnp.exp2(r2 * sums_r[r, j]) * now + in_r[x, half, r, j, i]
            return carry

        lax.fori_loop(0, HALF, scan_row, 0)
        copies = []
        for o, peer in enumerate(row_peers):
            copies.append(send(out_r.at[x, half, peer[0]], got_r.at[half, pl.ds(ri * kr, kr)],
                               b_out.at[x, half, o], b_in.at[x, half, o], peer))
        for p, peer in enumerate(col_peers):
            o = nr - 1 + p
            copies.append(send(out_c.at[x, half, peer[1]], got_c.at[half, pl.ds(ci * hc, hc)],
                               b_out.at[x, half, o], b_in.at[x, half, o], peer))
        got_r[half, pl.ds(ri * kr, kr)] = out_r[x, half, ri]
        got_c[half, pl.ds(ci * hc, hc)] = out_c[x, half, ci]
        return copies

    def arrive(copies):
        for copy in copies:
            copy.wait()

    local_leaves(0)
    pl.semaphore_wait(barrier, len(row_peers) + len(col_peers))
    one = scatter(0, 0, leave_v, leave_a)
    local_leaves(1)
    two = scatter(0, 1, leave_v, leave_a)
    one = give_back(0, 0, one, from_above, from_right)
    two = give_back(0, 1, two, from_above, from_right)
    arrive(one)
    carried_leaves(0)
    one = scatter(1, 0, leave_p, leave_s)
    arrive(two)
    carried_leaves(1)
    two = scatter(1, 1, leave_p, leave_s)
    one = give_back(1, 0, one, from_below, from_left)
    two = give_back(1, 1, two, from_below, from_left)
    arrive(one)
    arrive(two)


def channel_sums(products, selector, turn, out, base, cols):
    values = products[...]
    high = values.astype(BF16)
    low = (values - high.astype(F32)).astype(BF16)
    sums = jnp.dot(high, selector[...], preferred_element_type=F32)
    sums = sums + jnp.dot(low, selector[...], preferred_element_type=F32)
    for b in range(BLOCK):
        parts = split3(sums[b * cols : b * cols + cols, :NS], 1)
        turned = lax.dot_general(parts, turn, (((0,), (0,)), ((), ())),
                                 preferred_element_type=F32)
        out[base + b] = turned[:NS] + turned[NS : 2 * NS] + turned[2 * NS :]


def outputs_kernel(feat, step, grad, decay_log, from_above, from_right, from_left, from_below,
                   sum_cols, before, later, earlier, coded,
                   g_feat, g_step, g_write, g_read, g_decay,
                   rates, spreader, selector, drive, vert, below, kept_s, kept_v, products):
    rows, cols = step.shape[0], step.shape[1]
    K = cols // S
    set_rates(decay_log, rates)
    set_spreader(spreader)
    set_selector(selector)
    turn = by_segment(cols)
    vert[...] = from_above[...]
    below[...] = from_below[...]
    g_decay[...] = jnp.zeros_like(g_decay)
    slow = -jnp.exp(decay_log[...]) * LOG2E

    def forward(base, within, carry):
        h = base + within
        for k in range(K):
            drive[k] = column(step, h, k, K) * column(feat, h, k, K)
        ahead = before[h]
        only = coded[h, :cols, :]
        for pair in range(NS // 2):
            spreads = spread(only, spreader, pair)
            for j in range(2):
                n = 2 * pair + j
                half, i = divmod(n, HALF)
                r2 = rates[n]
                s = jnp.exp2(r2 * ahead) * (earlier[h, n] + from_left[half, h, i : i + 1, :])
                for k in range(K):
                    e = jnp.exp2(column(step, h, k, K) * r2)
                    q = e * vert[half, k, i]
                    v = q + drive[k] * tile_of(spreads, S * k, j)
                    vert[half, k, i] = v
                    t = e * s
                    s = t + v
                    kept_v[h, k, n] = q
                    kept_s[h, k, n] = t
                    products[pl.ds(cols * within + S * k, S), D * n : D * n + D] = (
                        s * column(grad, h, k, K))
        return carry

    def backward(base, back, carry):
        within = BLOCK - 1 - back
        h = base + within
        total = jnp.zeros((S, D), F32)
        for k in range(K):
            dt = column(step, h, k, K)
            drive[k] = dt * column(feat, h, k, K)
            total = total + dt
        upto = before[h] + total
        gone = jnp.exp2(slow * sum_cols[h])
        both = coded[h]
        through = [jnp.zeros((S, D), F32)] * K
        rated = [jnp.zeros((S, D), F32)] * K
        for pair in range(NS // 2):
            spreads = spread(both, spreader, pair)
            for j in range(2):
                n = 2 * pair + j
                half, i = divmod(n, HALF)
                r2 = rates[n]
                entering = gone[n : n + 1, :] * from_right[half, h, i : i + 1, :]
                a = jnp.exp2(-r2 * upto) * (later[h, n] + entering)
                stepped = jnp.zeros((S, D), F32)
                for k in reversed(range(K)):
                    dt = column(step, h, k, K)
                    e = jnp.exp2(dt * r2)
                    ah = a + tile_of(spreads, cols + S * k, j) * column(grad, h, k, K)
                    av = ah + below[half, k, i]
                    below[half, k, i] = e * av
                    a = e * ah
                    eg = ah * kept_s[h, k, n] + av * kept_v[h, k, n]
                    through[k] = through[k] + av * tile_of(spreads, S * k, j)
                    rated[k] = rated[k] + eg * r2
                    stepped = stepped + eg * dt
                    products[pl.ds(cols * within + S * k, S), D * n : D * n + D] = av * drive[k]
                g_decay[n] += stepped
        for k in range(K):
            g_feat[h, pl.ds(k, S, stride=K), :] = column(step, h, k, K) * through[k]
            g_step[h, pl.ds(k, S, stride=K), :] = (
                column(feat, h, k, K) * through[k] + LN2 * rated[k])
        return carry

    def forward_block(b, carry):
        lax.fori_loop(0, BLOCK, functools.partial(forward, b * BLOCK), 0)
        channel_sums(products, selector, turn, g_read, b * BLOCK, cols)
        return carry

    def backward_block(b, carry):
        base = rows - BLOCK - b * BLOCK
        lax.fori_loop(0, BLOCK, functools.partial(backward, base), 0)
        channel_sums(products, selector, turn, g_write, base, cols)
        return carry

    lax.fori_loop(0, rows // BLOCK, forward_block, 0)
    lax.fori_loop(0, rows // BLOCK, backward_block, 0)


def total_kernel(nr, nc, part, decay_log, out, by_row, by_col, s_out, s_in):
    ri, ci = lax.axis_index("row"), lax.axis_index("col")
    row_peers = [(lax.rem(ri + o, nr), ci) for o in range(1, nr)]
    col_peers = [(ri, lax.rem(ci + o, nc)) for o in range(1, nc)]
    barrier = pltpu.get_barrier_semaphore()
    for peer in row_peers + col_peers:
        pl.semaphore_signal(barrier, inc=1, device_id=peer, device_id_type=MESH)
    pl.semaphore_wait(barrier, len(row_peers) + len(col_peers))

    def stage(value, box, mine, peers, base):
        box[mine] = value
        copies = []
        for o, peer in enumerate(peers):
            copy = pltpu.make_async_remote_copy(
                src_ref=box.at[mine], dst_ref=box.at[mine], send_sem=s_out.at[base + o],
                recv_sem=s_in.at[base + o], device_id=peer, device_id_type=MESH)
            copy.start()
            copies.append(copy)
        for copy in copies:
            copy.wait()
        return jnp.sum(box[...], axis=0)

    value = stage(jnp.sum(part[...], axis=1), by_row, ri, row_peers, 0)
    value = stage(value, by_col, ci, col_peers, nr - 1)
    out[...] = value * -jnp.exp(decay_log[...])


def total(nr, nc, part, decay_log):
    dma = pltpu.SemaphoreType.DMA((nr + nc - 2,))
    return pl.pallas_call(
        functools.partial(total_kernel, nr, nc),
        out_shape=jax.ShapeDtypeStruct((NS, D), F32),
        in_specs=[VMEM] * 2,
        out_specs=VMEM,
        scratch_shapes=[pltpu.VMEM((nr, NS, D), F32), pltpu.VMEM((nc, NS, D), F32), dma, dma],
        compiler_params=pltpu.CompilerParams(
            collective_id=1, has_side_effects=True, vmem_limit_bytes=4 << 20),
        name="total",
    )(part, decay_log)


def shards(features, step_size, write_weights, read_weights, decay_log, out_grad):
    rows, cols = step_size.shape[0], step_size.shape[1]
    K = cols // S
    nr, nc = lax.axis_size("row"), lax.axis_size("col")
    kr, hc, peers = K // nr, rows // nc, nr + nc - 2
    sds = jax.ShapeDtypeStruct
    vm = pltpu.VMEM
    carry_r, carry_c = (2, K, HALF, S, D), (2, rows, HALF, D)
    rates, spreader = vm((NS, S, D), F32), vm((3 * NS, NS * D), BF16)
    drive = vm((K, S, D), F32)
    write_t, read_t = write_weights.transpose(0, 2, 1), read_weights.transpose(0, 2, 1)

    outs = [carry_r, carry_c, carry_c, carry_r, (rows, 1, D), (rows, S, D),
            (rows, NS, S, D), (rows, NS, S, D)]
    outs = [sds(o, F32) for o in outs] + [sds((rows, 2 * cols, 3 * NS), BF16)]
    args = (features, step_size, write_t, read_t, out_grad, decay_log)
    box_r, box_c = vm((2, 2, nr, kr, HALF, S, D), F32), vm((2, 2, nc, hc, HALF, D), F32)
    dma = pltpu.SemaphoreType.DMA((2, 2, peers))
    few = pltpu.SemaphoreType.DMA((peers,))
    passed = pl.pallas_call(
        functools.partial(carries_kernel, nr, nc),
        out_shape=outs,
        in_specs=[VMEM] * len(args),
        out_specs=[VMEM] * len(outs),
        scratch_shapes=[
            rates, spreader, drive, vm(carry_r, F32), vm(carry_r, F32), vm(carry_c, F32),
            vm(carry_r, F32), vm(carry_c, F32), vm((K, S, D), F32),
            vm((nr, kr, S, D), F32), vm((nc, hc, 1, D), F32),
            box_r, box_c, box_r, box_c, dma, dma, dma, dma, few, few],
        compiler_params=pltpu.CompilerParams(
            collective_id=0, has_side_effects=True, vmem_limit_bytes=30 << 20),
        name="carries",
    )(*args)

    args = (features, step_size, out_grad, decay_log) + tuple(passed)
    outs = [(rows, cols, D), (rows, cols, D), (rows, NS, cols), (rows, NS, cols), (NS, S, D)]
    g_feat, g_step, g_write, g_read, g_decay = pl.pallas_call(
        outputs_kernel,
        out_shape=[sds(o, F32) for o in outs],
        in_specs=[VMEM] * len(args),
        out_specs=[VMEM] * len(outs),
        scratch_shapes=[
            rates, spreader, vm((NS * D, D), BF16), drive, vm(carry_r, F32), vm(carry_r, F32),
            vm((rows, K, NS, S, D), F32), vm((rows, K, NS, S, D), F32),
            vm((BLOCK * cols, NS * D), F32)],
        compiler_params=pltpu.CompilerParams(vmem_limit_bytes=60 << 20),
        name="outputs",
    )(*args)
    g_decay = total(nr, nc, g_decay, decay_log)
    return (g_feat, g_step, g_write.transpose(0, 2, 1), g_read.transpose(0, 2, 1), g_decay)


def solution(mesh):
    tiles = P("row", "col", None)
    in_specs = (tiles, tiles, tiles, tiles, P(), tiles)
    out_specs = (tiles, tiles, tiles, tiles, P())
    return jax.shard_map(shards, mesh=mesh, in_specs=in_specs, out_specs=out_specs, check_vma=False)
```

```python
import functools
import math
import jax
import jax.numpy as jnp
from jax import lax
from jax.experimental import pallas as pl
from jax.experimental.pallas import tpu as pltpu
from jax.sharding import PartitionSpec as P

NS = 16
HALF = 8
D = 128
S = 8
F32 = jnp.float32
BF16 = jnp.bfloat16
LOG2E = math.log2(math.e)
LN2 = math.log(2.0)
MESH = pl.DeviceIdType.MESH
VMEM = pl.BlockSpec(memory_space=pltpu.VMEM)


def column(ref, h, k, width):
    return ref[h, pl.ds(k, S, stride=width), :]


def set_rates(decay_log, rates):
    for n in range(NS):
        rates[n] = jnp.broadcast_to(-jnp.exp(decay_log[n : n + 1, :]) * LOG2E, (S, D))


def equal(a, b):
    return jnp.where(a == b, 1.0, 0.0).astype(BF16)


def set_spreader(spreader):
    of = lax.broadcasted_iota(jnp.int32, spreader.shape, 0) % NS
    to = lax.broadcasted_iota(jnp.int32, spreader.shape, 1) // D
    spreader[...] = equal(of, to)


def by_segment(cols):
    K = cols // S
    at = lax.broadcasted_iota(jnp.int32, (cols, cols), 0)
    col = lax.broadcasted_iota(jnp.int32, (cols, cols), 1)
    return equal(col, (at % S) * K + at // S)


def split3(x, axis):
    high = x.astype(BF16)
    rest = x - high.astype(F32)
    mid = rest.astype(BF16)
    low = (rest - mid.astype(F32)).astype(BF16)
    return jnp.concatenate([high, mid, low], axis=axis)


def spread(coded, spreader, pair):
    return jnp.dot(coded, spreader[:, 2 * D * pair : 2 * D * pair + 2 * D],
                   preferred_element_type=F32)


def sublane():
    return lax.broadcasted_iota(jnp.int32, (S, D), 0)


def sums_down(value, at):
    for shift in (1, 2, 4):
        value = value + jnp.where(at >= shift, pltpu.roll(value, shift, 0), 0.0)
    return value


def tile_of(block, row, half):
    return block[row : row + S, D * half : D * half + D]


def states_of(half):
    return slice(half * HALF, half * HALF + HALF)


def add_sums(total, products, picker, n):
    values = products[n]
    high = values.astype(BF16)
    low = (values - high.astype(F32)).astype(BF16)
    return total + lax.dot_general(
        picker[n], jnp.concatenate([high, low], axis=1), (((1,), (1,)), ((), ())),
        preferred_element_type=F32)


def scan_kernel(nr, nc, feat, step, write, read, grad, decay_log,
                g_feat, g_step, g_write, g_read, g_decay,
                rates, slow, spreader, picker, coded, steps, grads, drive,
                before, upto, sum_cols, sum_rows, later, earlier, mix,
                leave_v, leave_p, vert, from_above, from_below,
                leave_a, leave_s, from_right, from_left, kept_s, kept_v, even, odd, part,
                sums_r, sums_c, in_v, out_v, in_p, out_p, in_a, out_a, in_s, out_s,
                by_row, by_col, row_sems, col_sems):
    rows, cols = step.shape[0], step.shape[1]
    K = cols // S
    ri, ci = lax.axis_index("row"), lax.axis_index("col")
    kr, hc = K // nr, rows // nc
    row_peers = [(lax.rem(ri + o, nr), ci) for o in range(1, nr)]
    col_peers = [(ri, lax.rem(ci + o, nc)) for o in range(1, nc)]
    barrier = pltpu.get_barrier_semaphore()
    for peer in row_peers + col_peers:
        pl.semaphore_signal(barrier, inc=1, device_id=peer, device_id_type=MESH)

    set_rates(decay_log, rates)
    set_spreader(spreader)
    slow[...] = -jnp.exp(decay_log[...]) * LOG2E
    picked = lax.broadcasted_iota(jnp.int32, picker.shape[1:], 0)
    for n in range(NS):
        picker[n] = equal(picked, n)
    leave_v[...] = jnp.zeros_like(leave_v)
    leave_p[...] = jnp.zeros_like(leave_p)
    sum_rows[...] = jnp.zeros_like(sum_rows)
    part[...] = jnp.zeros_like(part)
    at = sublane()
    turn = by_segment(cols)

    def code(h, carry):
        for i, ref in enumerate((write, read)):
            parts = split3(ref[h], 0)
            coded[h, cols * i : cols * i + cols, :] = lax.dot_general(
                turn, parts, (((1,), (1,)), ((), ())), preferred_element_type=F32).astype(BF16)
        return carry

    def over(lo, hi, row):
        def one(i, carry):
            row(i)
            return carry

        lax.fori_loop(lo, hi, one, 0)

    def local_vertical(half, h):
        if half == 0:
            total = jnp.zeros((S, D), F32)
            for k in range(K):
                dt = column(step, h, k, K)
                steps[h, k] = dt
                drive[h, k] = dt * column(feat, h, k, K)
                total = total + dt
                sum_rows[k] += dt
            ends = sums_down(total, at)
            upto[h] = ends
            before[h] = ends - total
            sum_cols[h] = ends[S - 1 :, :]
        only = coded[h, :cols, :]
        for pair in range(HALF // 2):
            spreads = spread(only, spreader, half * HALF // 2 + pair)
            for j in range(2):
                i = 2 * pair + j
                r2 = rates[half * HALF + i]
                for k in range(K):
                    e = jnp.exp2(steps[h, k] * r2)
                    leave_v[half, k, i] = (
                        e * leave_v[half, k, i] + drive[h, k] * tile_of(spreads, S * k, j))

    def local_adjoint(h):
        for k in range(K):
            grads[h, k] = column(grad, h, k, K)
        only = coded[h, cols:, :]
        ahead = before[h]
        for pair in range(NS // 2):
            spreads = spread(only, spreader, pair)
            for j in range(2):
                n = 2 * pair + j
                r2 = rates[n]
                a = jnp.zeros((S, D), F32)
                for k in reversed(range(K)):
                    e = jnp.exp2(steps[h, k] * r2)
                    a = e * (a + tile_of(spreads, S * k, j) * grads[h, k])
                mix[S * n : S * n + S, :] = jnp.exp2(r2 * ahead) * a
        for half in range(2):
            passed = jnp.zeros((HALF, D), F32)
            for g in reversed(range(S)):
                later[h, half, HALF * g : HALF * g + HALF, :] = passed
                passed = passed + mix[pl.ds(S * HALF * half + g, HALF, stride=S), :]
            leave_a[h, half] = passed

    def carried_states(h):
        only = coded[h, :cols, :]
        ends = upto[h]
        for pair in range(NS // 2):
            spreads = spread(only, spreader, pair)
            for j in range(2):
                n = 2 * pair + j
                half, i = divmod(n, HALF)
                r2 = rates[n]
                l = jnp.zeros((S, D), F32)
                for k in range(K):
                    e = jnp.exp2(steps[h, k] * r2)
                    v = e * vert[half, k, i] + drive[h, k] * tile_of(spreads, S * k, j)
                    vert[half, k, i] = v
                    l = e * l + v
                mix[S * n : S * n + S, :] = jnp.exp2(-r2 * ends) * l
        for half in range(2):
            passed = jnp.zeros((HALF, D), F32)
            for g in range(S):
                earlier[h, half, HALF * g : HALF * g + HALF, :] = passed
                passed = passed + mix[pl.ds(S * HALF * half + g, HALF, stride=S), :]
            leave_s[h, half] = jnp.exp2(slow[states_of(half), :] * sum_cols[h]) * passed

    def carried_adjoint(i):
        h = rows - 1 - i
        only = coded[h, cols:, :]
        ends = upto[h]
        for half in range(2):
            entering = jnp.exp2(slow[states_of(half), :] * sum_cols[h]) * from_right[h, half]
            for g in range(S):
                at_g = slice(HALF * g, HALF * g + HALF)
                later[h, half, at_g, :] = later[h, half, at_g, :] + entering
        for pair in range(NS // 2):
            spreads = spread(only, spreader, pair)
            for j in range(2):
                n = 2 * pair + j
                half, i = divmod(n, HALF)
                r2 = rates[n]
                a = jnp.exp2(-r2 * ends) * later[h, half, pl.ds(i, S, stride=HALF), :]
                for k in reversed(range(K)):
                    e = jnp.exp2(steps[h, k] * r2)
                    ah = a + tile_of(spreads, S * k, j) * grads[h, k]
                    leave_p[half, k, i] = e * (ah + leave_p[half, k, i])
                    a = e * ah

    def final_states(h, now, last):
        ahead = before[h]
        only = coded[h, :cols, :]
        for half in range(2):
            entering = from_left[h, half]
            for g in range(S):
                at_g = slice(HALF * g, HALF * g + HALF)
                earlier[h, half, at_g, :] = earlier[h, half, at_g, :] + entering
        sums = jnp.zeros((NS, cols), F32)
        for pair in range(NS // 2):
            spreads = spread(only, spreader, pair)
            for j in range(2):
                n = 2 * pair + j
                half, i = divmod(n, HALF)
                r2 = rates[n]
                s = jnp.exp2(r2 * ahead) * earlier[h, half, pl.ds(i, S, stride=HALF), :]
                for k in range(K):
                    e = jnp.exp2(steps[h, k] * r2)
                    q = e * from_above[half, k, i]
                    v = q + drive[h, k] * tile_of(spreads, S * k, j)
                    from_above[half, k, i] = v
                    t = e * s
                    s = t + v
                    kept_v[h, k, n] = q
                    kept_s[h, k, n] = t
                    now[n, pl.ds(k, S, stride=K), :] = s * grads[h, k]
                sums = add_sums(sums, last, picker, n)
        g_read[jnp.maximum(h - 1, 0)] = sums

    def final_adjoint(h, now, last):
        ends = upto[h]
        both = coded[h]
        through = [jnp.zeros((S, D), F32)] * K
        rated = [jnp.zeros((S, D), F32)] * K
        sums = jnp.zeros((NS, cols), F32)
        for pair in range(NS // 2):
            spreads = spread(both, spreader, pair)
            for j in range(2):
                n = 2 * pair + j
                half, i = divmod(n, HALF)
                r2 = rates[n]
                a = jnp.exp2(-r2 * ends) * later[h, half, pl.ds(i, S, stride=HALF), :]
                stepped = jnp.zeros((S, D), F32)
                for k in reversed(range(K)):
                    dt = steps[h, k]
                    e = jnp.exp2(dt * r2)
                    ah = a + tile_of(spreads, cols + S * k, j) * grads[h, k]
                    av = ah + from_below[half, k, i]
                    from_below[half, k, i] = e * av
                    a = e * ah
                    eg = ah * kept_s[h, k, n] + av * kept_v[h, k, n]
                    through[k] = through[k] + av * tile_of(spreads, S * k, j)
                    rated[k] = rated[k] + eg * r2
                    stepped = stepped + eg * dt
                    now[n, pl.ds(k, S, stride=K), :] = av * drive[h, k]
                part[n] += stepped
                sums = add_sums(sums, last, picker, n)
        g_write[jnp.minimum(h + 1, rows - 1)] = sums
        for k in range(K):
            g_feat[h, pl.ds(k, S, stride=K), :] = steps[h, k] * through[k]
            g_step[h, pl.ds(k, S, stride=K), :] = (
                column(feat, h, k, K) * through[k] + LN2 * rated[k])

    def states_pair(i):
        final_states(2 * i, even, odd)
        final_states(2 * i + 1, odd, even)

    def adjoint_pair(i):
        final_adjoint(rows - 1 - 2 * i, even, odd)
        final_adjoint(rows - 2 - 2 * i, odd, even)

    def last_sums():
        sums = jnp.zeros((NS, cols), F32)
        for n in range(NS):
            sums = add_sums(sums, odd, picker, n)
        return sums

    def send(src, dst, sems, kind, o, peer):
        copy = pltpu.make_async_remote_copy(
            src_ref=src, dst_ref=dst, send_sem=sems.at[kind, o], recv_sem=sems.at[kind + 1, o],
            device_id=peer, device_id_type=MESH)
        copy.start()
        return copy

    def arrive(copies):
        for copy in copies:
            copy.wait()

    mine_k, mine_h = pl.ds(ri * kr, kr), pl.ds(ci * hc, hc)

    def scatter_rows(source, box, kind):
        box[ri] = source(mine_k)[...]
        return [send(source(pl.ds(p[0] * kr, kr)), box.at[ri], row_sems, kind, o, p)
                for o, p in enumerate(row_peers)]

    def scatter_cols(source, box, kind):
        box[ci] = source(mine_h)[...]
        return [send(source(pl.ds(p[1] * hc, hc)), box.at[ci], col_sems, kind, o, p)
                for o, p in enumerate(col_peers)]

    def return_rows(box, target, kind):
        target(mine_k)[...] = box[ri]
        return [send(box.at[p[0]], target(mine_k), row_sems, kind, o, p)
                for o, p in enumerate(row_peers)]

    def return_cols(box, target, kind):
        target(mine_h)[...] = box[ci]
        return [send(box.at[p[1]], target(mine_h), col_sems, kind, o, p)
                for o, p in enumerate(col_peers)]

    def scan_cols(source, result, backward):
        for half in range(2):
            rate = slow[states_of(half), :]
            for j in range(hc):
                now = jnp.zeros((HALF, D), F32)
                for c in (reversed(range(nc)) if backward else range(nc)):
                    result[c, j, half] = now
                    now = jnp.exp2(rate * sums_c[c, j]) * now + source[c, j, half]

    lax.fori_loop(0, rows, code, 0, unroll=4)
    mid = rows // 2

    over(0, rows, functools.partial(local_vertical, 0))
    pl.semaphore_wait(barrier, len(row_peers) + len(col_peers))
    flights = [None, None]
    flights[0] = scatter_rows(lambda k: leave_v.at[0, k], in_v.at[0], 0)
    flights[0] += scatter_rows(lambda k: sum_rows.at[k], sums_r, 8)
    sum_flight = scatter_cols(lambda h: sum_cols.at[h], sums_c, 4)
    over(0, rows, functools.partial(local_vertical, 1))
    flights[1] = scatter_rows(lambda k: leave_v.at[1, k], in_v.at[1], 4)
    over(0, mid, local_adjoint)
    for half in range(2):
        arrive(flights[half])

        def scan_row(i, carry, half=half):
            r2 = rates[half * HALF + i]
            for j in range(kr):
                now = jnp.zeros((S, D), F32)
                for r in range(nr):
                    out_v[half, r, j, i] = now
                    now = jnp.exp2(r2 * sums_r[r, j]) * now + in_v[half, r, j, i]
            return carry

        lax.fori_loop(0, HALF, scan_row, 0)
        flights[half] = return_rows(out_v.at[half], lambda k: from_above.at[half, k], 2 + 4 * half)
    over(mid, rows, local_adjoint)
    right = scatter_cols(lambda h: leave_a.at[h], in_a, 0)
    arrive(flights[0])
    arrive(flights[1])
    vert[...] = from_above[...]
    over(0, mid, carried_states)
    arrive(sum_flight)
    arrive(right)
    scan_cols(in_a, out_a, True)
    right = return_cols(out_a, lambda h: from_right.at[h], 2)
    over(mid, rows, carried_states)
    left = scatter_cols(lambda h: leave_s.at[h], in_s, 6)
    arrive(right)
    over(0, mid, carried_adjoint)
    arrive(left)
    scan_cols(in_s, out_s, False)
    left = return_cols(out_s, lambda h: from_left.at[h], 8)
    over(mid, rows, carried_adjoint)
    under = scatter_rows(lambda k: leave_p.at[:, k], in_p, 10)
    arrive(left)
    over(0, mid // 2, states_pair)
    arrive(under)

    def scan_up(i, carry):
        for half in range(2):
            r2 = rates[half * HALF + i]
            for j in range(kr):
                now = jnp.zeros((S, D), F32)
                for r in reversed(range(nr)):
                    out_p[r, half, j, i] = now
                    now = jnp.exp2(r2 * sums_r[r, j]) * now + in_p[r, half, j, i]
        return carry

    lax.fori_loop(0, HALF, scan_up, 0)
    under = return_rows(out_p, lambda k: from_below.at[:, k], 12)
    over(mid // 2, mid, states_pair)
    g_read[rows - 1] = last_sums()
    arrive(under)
    over(0, mid, adjoint_pair)

    by_row[ri] = jnp.sum(part[...], axis=1)
    arrive([send(by_row.at[ri], by_row.at[ri], row_sems, 14, o, p)
            for o, p in enumerate(row_peers)])
    by_col[ci] = jnp.sum(by_row[...], axis=0)
    flight = [send(by_col.at[ci], by_col.at[ci], col_sems, 10, o, p)
              for o, p in enumerate(col_peers)]
    g_write[0] = last_sums()
    arrive(flight)
    g_decay[...] = jnp.sum(by_col[...], axis=0) * -jnp.exp(decay_log[...])


def shards(features, step_size, write_weights, read_weights, decay_log, out_grad):
    rows, cols = step_size.shape[0], step_size.shape[1]
    K = cols // S
    nr, nc = lax.axis_size("row"), lax.axis_size("col")
    kr, hc = K // nr, rows // nc

    def vm(*shape, kind=F32):
        return pltpu.VMEM(shape, kind)

    carry_r, carry_c = vm(2, K, HALF, S, D), vm(rows, 2, HALF, D)
    grid, kept = vm(rows, K, S, D), vm(rows, K, NS, S, D)
    joined = vm(rows, 2, S * HALF, D)
    box_v, box_p = vm(2, nr, kr, HALF, S, D), vm(nr, 2, kr, HALF, S, D)
    box_c = vm(nc, hc, 2, HALF, D)
    args = (features, step_size, write_weights.transpose(0, 2, 1),
            read_weights.transpose(0, 2, 1), out_grad, decay_log)
    outs = [(rows, cols, D), (rows, cols, D), (rows, NS, cols), (rows, NS, cols), (NS, D)]
    g_feat, g_step, g_write, g_read, g_decay = pl.pallas_call(
        functools.partial(scan_kernel, nr, nc),
        out_shape=[jax.ShapeDtypeStruct(o, F32) for o in outs],
        in_specs=[VMEM] * len(args),
        out_specs=[VMEM] * len(outs),
        scratch_shapes=[
            vm(NS, S, D), vm(NS, D), vm(3 * NS, NS * D, kind=BF16), vm(NS, NS, 2 * D, kind=BF16),
            vm(rows, 2 * cols, 3 * NS, kind=BF16), grid, grid, grid,
            vm(rows, S, D), vm(rows, S, D), vm(rows, 1, D), vm(K, S, D), joined, joined,
            vm(NS * S, D),
            carry_r, carry_r, carry_r, carry_r, carry_r,
            carry_c, carry_c, carry_c, carry_c, kept, kept,
            vm(NS, cols, D), vm(NS, cols, D), vm(NS, S, D),
            vm(nr, kr, S, D), vm(nc, hc, 1, D), box_v, box_v, box_p, box_p,
            box_c, box_c, box_c, box_c, vm(nr, NS, D), vm(nc, NS, D),
            pltpu.SemaphoreType.DMA((16, nr - 1)), pltpu.SemaphoreType.DMA((12, nc - 1))],
        compiler_params=pltpu.CompilerParams(
            collective_id=0, has_side_effects=True, vmem_limit_bytes=57 << 20),
        name="scan",
    )(*args)
    return (g_feat, g_step, g_write.transpose(0, 2, 1), g_read.transpose(0, 2, 1), g_decay)


def solution(mesh):
    tiles = P("row", "col", None)
    in_specs = (tiles, tiles, tiles, tiles, P(), tiles)
    out_specs = (tiles, tiles, tiles, tiles, P())
    return jax.shard_map(shards, mesh=mesh, in_specs=in_specs, out_specs=out_specs, check_vma=False)
```

```python
import functools
import math
import jax
import jax.numpy as jnp
from jax import lax
from jax.experimental import pallas as pl
from jax.experimental.pallas import tpu as pltpu
from jax.sharding import PartitionSpec as P

NS = 16
HALF = 8
D = 128
S = 8
F32 = jnp.float32
BF16 = jnp.bfloat16
LOG2E = math.log2(math.e)
LN2 = math.log(2.0)
MESH = pl.DeviceIdType.MESH
VMEM = pl.BlockSpec(memory_space=pltpu.VMEM)


def column(ref, h, k, width):
    return ref[h, pl.ds(k, S, stride=width), :]


def set_rates(decay_log, rates):
    for n in range(NS):
        rates[n] = jnp.broadcast_to(-jnp.exp(decay_log[n : n + 1, :]) * LOG2E, (S, D))


def equal(a, b):
    return jnp.where(a == b, 1.0, 0.0).astype(BF16)


def set_spreaders(writes, reads, both):
    for table, parts in ((writes, (0,)), (reads, (1,)), (both, (0, 1))):
        row = lax.broadcasted_iota(jnp.int32, table.shape, 0)
        to = lax.broadcasted_iota(jnp.int32, table.shape, 1) // D
        if len(parts) == 1:
            meets = jnp.where(row // (3 * NS) == parts[0], row % NS, NS) == to
        else:
            meets = 2 * (row % NS) + row // (3 * NS) == to
        table[...] = jnp.where(meets, 1.0, 0.0).astype(BF16)


def by_segment(cols):
    K = cols // S
    at = lax.broadcasted_iota(jnp.int32, (cols, cols), 0)
    col = lax.broadcasted_iota(jnp.int32, (cols, cols), 1)
    return equal(col, (at % S) * K + at // S)


def split3(x, axis):
    high = x.astype(BF16)
    rest = x - high.astype(F32)
    mid = rest.astype(BF16)
    low = (rest - mid.astype(F32)).astype(BF16)
    return jnp.concatenate([high, mid, low], axis=axis)


def spread(coded, table, at):
    return jnp.dot(coded, table[:, 2 * D * at : 2 * D * at + 2 * D],
                   preferred_element_type=F32)


def sublane():
    return lax.broadcasted_iota(jnp.int32, (S, D), 0)


def sums_down(value, at):
    for shift in (1, 2, 4):
        value = value + jnp.where(at >= shift, pltpu.roll(value, shift, 0), 0.0)
    return value


def tile_of(block, row, half):
    return block[row : row + S, D * half : D * half + D]


def states_of(half):
    return slice(half * HALF, half * HALF + HALF)


def channel_sums(values, picker, n):
    high = values.astype(BF16)
    low = (values - high.astype(F32)).astype(BF16)
    return lax.dot_general(
        picker[n], jnp.concatenate([high, low], axis=1), (((1,), (1,)), ((), ())),
        preferred_element_type=F32)


def scan_kernel(nr, nc, feat, step, write, read, grad, decay_log,
                g_feat, g_step, g_write, g_read, g_decay,
                rates, slow, writes, reads, both, picker, coded, steps, grads, drive,
                before, upto, sum_cols, sum_rows, later, earlier, mix,
                leave_v, leave_p, vert, from_above, from_below,
                leave_a, leave_s, from_right, from_left, kept_s, kept_v, products, part,
                sums_r, sums_c, in_v, out_v, in_p, out_p, in_a, out_a, in_s, out_s,
                by_row, by_col, row_sems, col_sems):
    rows, cols = step.shape[0], step.shape[1]
    K = cols // S
    mid = rows // 2
    ri, ci = lax.axis_index("row"), lax.axis_index("col")
    kr, hc = K // nr, rows // nc
    row_peers = [(lax.rem(ri + o, nr), ci) for o in range(1, nr)]
    col_peers = [(ri, lax.rem(ci + o, nc)) for o in range(1, nc)]
    barrier = pltpu.get_barrier_semaphore()
    for peer in row_peers + col_peers:
        pl.semaphore_signal(barrier, inc=1, device_id=peer, device_id_type=MESH)

    set_rates(decay_log, rates)
    set_spreaders(writes, reads, both)
    slow[...] = -jnp.exp(decay_log[...]) * LOG2E
    picked = lax.broadcasted_iota(jnp.int32, picker.shape[1:], 0)
    for n in range(NS):
        picker[n] = equal(picked, n)
    leave_v[...] = jnp.zeros_like(leave_v)
    leave_p[...] = jnp.zeros_like(leave_p)
    sum_rows[...] = jnp.zeros_like(sum_rows)
    part[...] = jnp.zeros_like(part)
    at = sublane()
    turn = by_segment(cols)

    def code(h, carry):
        parts = jnp.concatenate([split3(write[h], 0), split3(read[h], 0)], axis=0)
        coded[pl.ds(pl.multiple_of(h * cols, cols), cols), :] = lax.dot_general(
            turn, parts, (((1,), (1,)), ((), ())), preferred_element_type=F32).astype(BF16)
        return carry

    def two_rows(i):
        return coded[pl.ds(pl.multiple_of(2 * cols * i, 2 * cols), 2 * cols), :]

    def each_state(codes, table, lo, hi):
        for pair in range(lo // 2, hi // 2):
            spreads = spread(codes, table, pair)
            for j in range(2):
                n = 2 * pair + j
                half, i = divmod(n, HALF)
                yield n, half, i, [
                    [tile_of(spreads, cols * u + S * k, j) for k in range(K)] for u in range(2)]

    def over(lo, hi, row):
        def one(i, carry):
            row(i)
            return carry

        lax.fori_loop(lo, hi, one, 0)

    def local_vertical(half, at_pair):
        pair = (2 * at_pair, 2 * at_pair + 1)
        if half == 0:
            for h in pair:
                total = jnp.zeros((S, D), F32)
                for k in range(K):
                    dt = column(step, h, k, K)
                    steps[h, k] = dt
                    drive[h, k] = dt * column(feat, h, k, K)
                    total = total + dt
                    sum_rows[k] += dt
                ends = sums_down(total, at)
                upto[h] = ends
                before[h] = ends - total
                sum_cols[h] = ends[S - 1 :, :]
        for n, _, i, wb in each_state(two_rows(at_pair), writes, half * HALF, half * HALF + HALF):
            r2 = rates[n]
            for k in range(K):
                v = leave_v[half, k, i]
                for u, h in enumerate(pair):
                    v = jnp.exp2(steps[h, k] * r2) * v + drive[h, k] * wb[u][k]
                leave_v[half, k, i] = v

    def local_adjoint(at_pair):
        pair = (2 * at_pair, 2 * at_pair + 1)
        for h in pair:
            for k in range(K):
                grads[h, k] = column(grad, h, k, K)
        for n, _, _, rb in each_state(two_rows(at_pair), reads, 0, NS):
            r2 = rates[n]
            for u, h in enumerate(pair):
                a = jnp.zeros((S, D), F32)
                for k in reversed(range(K)):
                    a = jnp.exp2(steps[h, k] * r2) * (a + rb[u][k] * grads[h, k])
                mix[u, S * n : S * n + S, :] = jnp.exp2(r2 * before[h]) * a
        for u, h in enumerate(pair):
            for half in range(2):
                passed = jnp.zeros((HALF, D), F32)
                for g in reversed(range(S)):
                    later[h, half, HALF * g : HALF * g + HALF, :] = passed
                    passed = passed + mix[u, pl.ds(S * HALF * half + g, HALF, stride=S), :]
                leave_a[h, half] = passed

    def carried_states(at_pair):
        pair = (2 * at_pair, 2 * at_pair + 1)
        for n, half, i, wb in each_state(two_rows(at_pair), writes, 0, NS):
            r2 = rates[n]
            l = [jnp.zeros((S, D), F32)] * 2
            for k in range(K):
                v = vert[half, k, i]
                for u, h in enumerate(pair):
                    e = jnp.exp2(steps[h, k] * r2)
                    v = e * v + drive[h, k] * wb[u][k]
                    l[u] = e * l[u] + v
                vert[half, k, i] = v
            for u, h in enumerate(pair):
                mix[u, S * n : S * n + S, :] = jnp.exp2(-r2 * upto[h]) * l[u]
        for u, h in enumerate(pair):
            for half in range(2):
                passed = jnp.zeros((HALF, D), F32)
                for g in range(S):
                    earlier[h, half, HALF * g : HALF * g + HALF, :] = passed
                    passed = passed + mix[u, pl.ds(S * HALF * half + g, HALF, stride=S), :]
                leave_s[h, half] = jnp.exp2(slow[states_of(half), :] * sum_cols[h]) * passed

    def enter(joined, h, half, entering):
        for g in range(S):
            at_g = slice(HALF * g, HALF * g + HALF)
            joined[h, half, at_g, :] = joined[h, half, at_g, :] + entering

    def carried_adjoint(i):
        at_pair = mid - 1 - i
        pair = (2 * at_pair, 2 * at_pair + 1)
        for h in pair:
            for half in range(2):
                enter(later, h, half,
                      jnp.exp2(slow[states_of(half), :] * sum_cols[h]) * from_right[h, half])
        for n, half, i, rb in each_state(two_rows(at_pair), reads, 0, NS):
            r2 = rates[n]
            a = [jnp.exp2(-r2 * upto[h]) * later[h, half, pl.ds(i, S, stride=HALF), :]
                 for h in pair]
            for k in reversed(range(K)):
                p = leave_p[half, k, i]
                for u in (1, 0):
                    h = pair[u]
                    e = jnp.exp2(steps[h, k] * r2)
                    ah = a[u] + rb[u][k] * grads[h, k]
                    p = e * (ah + p)
                    a[u] = e * ah
                leave_p[half, k, i] = p

    def store_sums(out, at_pair, sums):
        out[2 * at_pair] = sums[:, :cols]
        out[2 * at_pair + 1] = sums[:, cols:]

    def final_states(at_pair):
        pair = (2 * at_pair, 2 * at_pair + 1)
        for h in pair:
            for half in range(2):
                enter(earlier, h, half, from_left[h, half])
        sums = jnp.zeros((NS, 2 * cols), F32)
        for n, half, i, wb in each_state(two_rows(at_pair), writes, 0, NS):
            sums = sums + channel_sums(products[n], picker, n)
            r2 = rates[n]
            s = [jnp.exp2(r2 * before[h]) * earlier[h, half, pl.ds(i, S, stride=HALF), :]
                 for h in pair]
            for k in range(K):
                v = from_above[half, k, i]
                for u, h in enumerate(pair):
                    e = jnp.exp2(steps[h, k] * r2)
                    q = e * v
                    v = q + drive[h, k] * wb[u][k]
                    t = e * s[u]
                    s[u] = t + v
                    kept_v[h, k, n] = q
                    kept_s[h, k, n] = t
                    products[n, pl.ds(cols * u + k, S, stride=K), :] = s[u] * grads[h, k]
                from_above[half, k, i] = v
        store_sums(g_read, jnp.maximum(at_pair - 1, 0), sums)

    def final_adjoint(i):
        at_pair = mid - 1 - i
        pair = (2 * at_pair, 2 * at_pair + 1)
        codes = two_rows(at_pair)
        through = [[jnp.zeros((S, D), F32)] * K for _ in range(2)]
        rated = [[jnp.zeros((S, D), F32)] * K for _ in range(2)]
        sums = jnp.zeros((NS, 2 * cols), F32)
        for n in range(NS):
            half, i = divmod(n, HALF)
            spreads = spread(codes, both, n)
            sums = sums + channel_sums(products[n], picker, n)
            r2 = rates[n]
            a = [jnp.exp2(-r2 * upto[h]) * later[h, half, pl.ds(i, S, stride=HALF), :]
                 for h in pair]
            stepped = jnp.zeros((S, D), F32)
            for k in reversed(range(K)):
                b = from_below[half, k, i]
                for u in (1, 0):
                    h = pair[u]
                    dt = steps[h, k]
                    e = jnp.exp2(dt * r2)
                    ah = a[u] + tile_of(spreads, cols * u + S * k, 1) * grads[h, k]
                    av = ah + b
                    b = e * av
                    a[u] = e * ah
                    eg = ah * kept_s[h, k, n] + av * kept_v[h, k, n]
                    through[u][k] = through[u][k] + av * tile_of(spreads, cols * u + S * k, 0)
                    rated[u][k] = rated[u][k] + eg * r2
                    stepped = stepped + eg * dt
                    products[n, pl.ds(cols * u + k, S, stride=K), :] = av * drive[h, k]
                from_below[half, k, i] = b
            part[n] += stepped
        store_sums(g_write, jnp.minimum(at_pair + 1, mid - 1), sums)
        for u, h in enumerate(pair):
            for k in range(K):
                g_feat[h, pl.ds(k, S, stride=K), :] = steps[h, k] * through[u][k]
                g_step[h, pl.ds(k, S, stride=K), :] = (
                    column(feat, h, k, K) * through[u][k] + LN2 * rated[u][k])

    def last_sums():
        sums = jnp.zeros((NS, 2 * cols), F32)
        for n in range(NS):
            sums = sums + channel_sums(products[n], picker, n)
        return sums

    def send(src, dst, sems, kind, o, peer):
        copy = pltpu.make_async_remote_copy(
            src_ref=src, dst_ref=dst, send_sem=sems.at[kind, o], recv_sem=sems.at[kind + 1, o],
            device_id=peer, device_id_type=MESH)
        copy.start()
        return copy

    def arrive(copies):
        for copy in copies:
            copy.wait()

    mine_k, mine_h = pl.ds(ri * kr, kr), pl.ds(ci * hc, hc)

    def scatter_rows(source, box, kind):
        box[ri] = source(mine_k)[...]
        return [send(source(pl.ds(p[0] * kr, kr)), box.at[ri], row_sems, kind, o, p)
                for o, p in enumerate(row_peers)]

    def scatter_cols(source, box, kind):
        box[ci] = source(mine_h)[...]
        return [send(source(pl.ds(p[1] * hc, hc)), box.at[ci], col_sems, kind, o, p)
                for o, p in enumerate(col_peers)]

    def return_rows(box, target, kind):
        target(mine_k)[...] = box[ri]
        return [send(box.at[p[0]], target(mine_k), row_sems, kind, o, p)
                for o, p in enumerate(row_peers)]

    def return_cols(box, target, kind):
        target(mine_h)[...] = box[ci]
        return [send(box.at[p[1]], target(mine_h), col_sems, kind, o, p)
                for o, p in enumerate(col_peers)]

    def scan_cols(source, result, backward):
        for half in range(2):
            rate = slow[states_of(half), :]
            for j in range(hc):
                now = jnp.zeros((HALF, D), F32)
                for c in (reversed(range(nc)) if backward else range(nc)):
                    result[c, j, half] = now
                    now = jnp.exp2(rate * sums_c[c, j]) * now + source[c, j, half]

    lax.fori_loop(0, rows, code, 0, unroll=4)
    part_way = mid // 2

    over(0, mid, functools.partial(local_vertical, 0))
    pl.semaphore_wait(barrier, len(row_peers) + len(col_peers))
    flights = [None, None]
    flights[0] = scatter_rows(lambda k: leave_v.at[0, k], in_v.at[0], 0)
    flights[0] += scatter_rows(lambda k: sum_rows.at[k], sums_r, 8)
    sum_flight = scatter_cols(lambda h: sum_cols.at[h], sums_c, 4)
    over(0, mid, functools.partial(local_vertical, 1))
    flights[1] = scatter_rows(lambda k: leave_v.at[1, k], in_v.at[1], 4)
    over(0, part_way, local_adjoint)
    for half in range(2):
        arrive(flights[half])

        def scan_row(i, carry, half=half):
            r2 = rates[half * HALF + i]
            for j in range(kr):
                now = jnp.zeros((S, D), F32)
                for r in range(nr):
                    out_v[half, r, j, i] = now
                    now = jnp.exp2(r2 * sums_r[r, j]) * now + in_v[half, r, j, i]
            return carry

        lax.fori_loop(0, HALF, scan_row, 0)
        flights[half] = return_rows(out_v.at[half], lambda k: from_above.at[half, k], 2 + 4 * half)
    over(part_way, mid, local_adjoint)
    right = scatter_cols(lambda h: leave_a.at[h], in_a, 0)
    arrive(flights[0])
    arrive(flights[1])
    vert[...] = from_above[...]
    over(0, part_way, carried_states)
    arrive(sum_flight)
    arrive(right)
    scan_cols(in_a, out_a, True)
    right = return_cols(out_a, lambda h: from_right.at[h], 2)
    over(part_way, mid, carried_states)
    left = scatter_cols(lambda h: leave_s.at[h], in_s, 6)
    arrive(right)
    over(0, part_way, carried_adjoint)
    arrive(left)
    scan_cols(in_s, out_s, False)
    left = return_cols(out_s, lambda h: from_left.at[h], 8)
    over(part_way, mid, carried_adjoint)
    under = scatter_rows(lambda k: leave_p.at[:, k], in_p, 10)
    arrive(left)
    over(0, part_way, final_states)
    arrive(under)

    def scan_up(i, carry):
        for half in range(2):
            r2 = rates[half * HALF + i]
            for j in range(kr):
                now = jnp.zeros((S, D), F32)
                for r in reversed(range(nr)):
                    out_p[r, half, j, i] = now
                    now = jnp.exp2(r2 * sums_r[r, j]) * now + in_p[r, half, j, i]
        return carry

    lax.fori_loop(0, HALF, scan_up, 0)
    under = return_rows(out_p, lambda k: from_below.at[:, k], 12)
    over(part_way, mid, final_states)
    store_sums(g_read, mid - 1, last_sums())
    arrive(under)
    over(0, mid, final_adjoint)

    by_row[ri] = jnp.sum(part[...], axis=1)
    arrive([send(by_row.at[ri], by_row.at[ri], row_sems, 14, o, p)
            for o, p in enumerate(row_peers)])
    by_col[ci] = jnp.sum(by_row[...], axis=0)
    flight = [send(by_col.at[ci], by_col.at[ci], col_sems, 10, o, p)
              for o, p in enumerate(col_peers)]
    store_sums(g_write, 0, last_sums())
    arrive(flight)
    g_decay[...] = jnp.sum(by_col[...], axis=0) * -jnp.exp(decay_log[...])


def shards(features, step_size, write_weights, read_weights, decay_log, out_grad):
    rows, cols = step_size.shape[0], step_size.shape[1]
    K = cols // S
    nr, nc = lax.axis_size("row"), lax.axis_size("col")
    kr, hc = K // nr, rows // nc

    def vm(*shape, kind=F32):
        return pltpu.VMEM(shape, kind)

    carry_r, carry_c = vm(2, K, HALF, S, D), vm(rows, 2, HALF, D)
    grid, kept = vm(rows, K, S, D), vm(rows, K, NS, S, D)
    joined = vm(rows, 2, S * HALF, D)
    box_v, box_p = vm(2, nr, kr, HALF, S, D), vm(nr, 2, kr, HALF, S, D)
    table = vm(6 * NS, NS * D, kind=BF16)
    box_c = vm(nc, hc, 2, HALF, D)
    args = (features, step_size, write_weights.transpose(0, 2, 1),
            read_weights.transpose(0, 2, 1), out_grad, decay_log)
    outs = [(rows, cols, D), (rows, cols, D), (rows, NS, cols), (rows, NS, cols), (NS, D)]
    g_feat, g_step, g_write, g_read, g_decay = pl.pallas_call(
        functools.partial(scan_kernel, nr, nc),
        out_shape=[jax.ShapeDtypeStruct(o, F32) for o in outs],
        in_specs=[VMEM] * len(args),
        out_specs=[VMEM] * len(outs),
        scratch_shapes=[
            vm(NS, S, D), vm(NS, D), table, table, vm(6 * NS, 2 * NS * D, kind=BF16),
            vm(NS, NS, 2 * D, kind=BF16), vm(rows * cols, 6 * NS, kind=BF16), grid, grid, grid,
            vm(rows, S, D), vm(rows, S, D), vm(rows, 1, D), vm(K, S, D), joined, joined,
            vm(2, NS * S, D),
            carry_r, carry_r, carry_r, carry_r, carry_r,
            carry_c, carry_c, carry_c, carry_c, kept, kept,
            vm(NS, 2 * cols, D), vm(NS, S, D),
            vm(nr, kr, S, D), vm(nc, hc, 1, D), box_v, box_v, box_p, box_p,
            box_c, box_c, box_c, box_c, vm(nr, NS, D), vm(nc, NS, D),
            pltpu.SemaphoreType.DMA((16, nr - 1)), pltpu.SemaphoreType.DMA((12, nc - 1))],
        compiler_params=pltpu.CompilerParams(
            collective_id=0, has_side_effects=True, vmem_limit_bytes=57 << 20),
        name="scan",
    )(*args)
    return (g_feat, g_step, g_write.transpose(0, 2, 1), g_read.transpose(0, 2, 1), g_decay)


def solution(mesh):
    tiles = P("row", "col", None)
    in_specs = (tiles, tiles, tiles, tiles, P(), tiles)
    out_specs = (tiles, tiles, tiles, tiles, P())
    return jax.shard_map(shards, mesh=mesh, in_specs=in_specs, out_specs=out_specs, check_vma=False)
```

```python
import functools
import math
import jax
import jax.numpy as jnp
from jax import lax
from jax.experimental import pallas as pl
from jax.experimental.pallas import tpu as pltpu
from jax.sharding import PartitionSpec as P

NS = 16
HALF = 8
D = 128
S = 8
F32 = jnp.float32
BF16 = jnp.bfloat16
LOG2E = math.log2(math.e)
LN2 = math.log(2.0)
MESH = pl.DeviceIdType.MESH
VMEM = pl.BlockSpec(memory_space=pltpu.VMEM)


def column(ref, h, k, width):
    return ref[h, pl.ds(k, S, stride=width), :]


def set_rates(decay_log, rates):
    for n in range(NS):
        rates[n] = jnp.broadcast_to(-jnp.exp(decay_log[n : n + 1, :]) * LOG2E, (S, D))


def equal(a, b):
    return jnp.where(a == b, 1.0, 0.0).astype(BF16)


def set_spreaders(writes, reads, both):
    for table, parts in ((writes, (0,)), (reads, (1,)), (both, (0, 1))):
        row = lax.broadcasted_iota(jnp.int32, table.shape, 0)
        to = lax.broadcasted_iota(jnp.int32, table.shape, 1) // D
        if len(parts) == 1:
            meets = jnp.where(row // (3 * NS) == parts[0], row % NS, NS) == to
        else:
            meets = 2 * (row % NS) + row // (3 * NS) == to
        table[...] = jnp.where(meets, 1.0, 0.0).astype(BF16)


def by_segment(cols):
    K = cols // S
    at = lax.broadcasted_iota(jnp.int32, (cols, cols), 0)
    col = lax.broadcasted_iota(jnp.int32, (cols, cols), 1)
    return equal(col, (at % S) * K + at // S)


def split3(x, axis):
    high = x.astype(BF16)
    rest = x - high.astype(F32)
    mid = rest.astype(BF16)
    low = (rest - mid.astype(F32)).astype(BF16)
    return jnp.concatenate([high, mid, low], axis=axis)


def spread(coded, table, at):
    return jnp.dot(coded, table[:, 2 * D * at : 2 * D * at + 2 * D],
                   preferred_element_type=F32)


def sublane():
    return lax.broadcasted_iota(jnp.int32, (S, D), 0)


def sums_down(value, at):
    for shift in (1, 2, 4):
        value = value + jnp.where(at >= shift, pltpu.roll(value, shift, 0), 0.0)
    return value


def tile_of(block, row, half):
    return block[row : row + S, D * half : D * half + D]


def states_of(half):
    return slice(half * HALF, half * HALF + HALF)


def channel_sums(values, picker, n):
    high = values.astype(BF16)
    low = (values - high.astype(F32)).astype(BF16)
    return lax.dot_general(
        picker[n], jnp.concatenate([high, low], axis=1), (((1,), (1,)), ((), ())),
        preferred_element_type=F32)


def scan_kernel(nr, nc, feat, step, write, read, grad_far, decay_log,
                g_feat, g_step, g_write, g_read, g_decay,
                rates, slow, writes, reads, both, picker, coded, steps, grads, drive,
                before, upto, sum_cols, sum_rows, later, earlier,
                leave_v, leave_p, from_above, from_below,
                leave_a, leave_s, from_right, from_left, kept_s, kept_v, products, part,
                sums_r, sums_c, in_r, out_r, in_c, out_c,
                by_row, by_col, grad, row_sems, col_sems, grad_sem):
    rows, cols = step.shape[0], step.shape[1]
    K = cols // S
    mid = rows // 2
    ri, ci = lax.axis_index("row"), lax.axis_index("col")
    kr, hc = K // nr, rows // nc
    row_peers = [(lax.rem(ri + o, nr), ci) for o in range(1, nr)]
    col_peers = [(ri, lax.rem(ci + o, nc)) for o in range(1, nc)]
    fetch = pltpu.make_async_copy(grad_far, grad, grad_sem)
    fetch.start()
    barrier = pltpu.get_barrier_semaphore()
    for peer in row_peers + col_peers:
        pl.semaphore_signal(barrier, inc=1, device_id=peer, device_id_type=MESH)

    set_rates(decay_log, rates)
    set_spreaders(writes, reads, both)
    slow[...] = -jnp.exp(decay_log[...]) * LOG2E
    picked = lax.broadcasted_iota(jnp.int32, picker.shape[1:], 0)
    for n in range(NS):
        picker[n] = equal(picked, n)
    leave_v[...] = jnp.zeros_like(leave_v)
    leave_p[...] = jnp.zeros_like(leave_p)
    sum_rows[...] = jnp.zeros_like(sum_rows)
    part[...] = jnp.zeros_like(part)
    at = sublane()
    turn = by_segment(cols)

    def code(h, carry):
        parts = jnp.concatenate([split3(write[h], 0), split3(read[h], 0)], axis=0)
        coded[pl.ds(pl.multiple_of(h * cols, cols), cols), :] = lax.dot_general(
            turn, parts, (((1,), (1,)), ((), ())), preferred_element_type=F32).astype(BF16)
        return carry

    def two_rows(i):
        return coded[pl.ds(pl.multiple_of(2 * cols * i, 2 * cols), 2 * cols), :]

    def set_drive(pair):
        for u, h in enumerate(pair):
            for k in range(K):
                drive[u, k] = steps[h, k] * column(feat, h, k, K)

    def each_state(codes, table, lo, hi):
        for pair in range(lo // 2, hi // 2):
            spreads = spread(codes, table, pair)
            for j in range(2):
                n = 2 * pair + j
                half, i = divmod(n, HALF)
                yield n, half, i, [
                    [tile_of(spreads, cols * u + S * k, j) for k in range(K)] for u in range(2)]

    def over(lo, hi, row):
        def one(i, carry):
            row(i)
            return carry

        lax.fori_loop(lo, hi, one, 0)

    def local_vertical(half, at_pair):
        pair = (2 * at_pair, 2 * at_pair + 1)
        if half == 0:
            for h in pair:
                total = jnp.zeros((S, D), F32)
                for k in range(K):
                    dt = column(step, h, k, K)
                    steps[h, k] = dt
                    total = total + dt
                    sum_rows[k] += dt
                ends = sums_down(total, at)
                upto[h] = ends
                before[h] = ends - total
                sum_cols[h] = ends[S - 1 :, :]
        set_drive(pair)
        for n, _, i, wb in each_state(two_rows(at_pair), writes, half * HALF, half * HALF + HALF):
            r2 = rates[n]
            for k in range(K):
                v = leave_v[half, k, i]
                for u, h in enumerate(pair):
                    v = jnp.exp2(steps[h, k] * r2) * v + drive[u, k] * wb[u][k]
                leave_v[half, k, i] = v

    def local_adjoint(at_pair):
        pair = (2 * at_pair, 2 * at_pair + 1)
        for h in pair:
            for k in range(K):
                grads[h, k] = column(grad, h, k, K)
        for n, _, _, rb in each_state(two_rows(at_pair), reads, 0, NS):
            r2 = rates[n]
            for u, h in enumerate(pair):
                a = jnp.zeros((S, D), F32)
                for k in reversed(range(K)):
                    a = jnp.exp2(steps[h, k] * r2) * (a + rb[u][k] * grads[h, k])
                products[u, S * n : S * n + S, :] = jnp.exp2(r2 * before[h]) * a
        for u, h in enumerate(pair):
            for half in range(2):
                passed = jnp.zeros((HALF, D), F32)
                for g in reversed(range(S)):
                    later[h, half, HALF * g : HALF * g + HALF, :] = passed
                    passed = passed + products[u, pl.ds(S * HALF * half + g, HALF, stride=S), :]
                leave_a[h, half] = passed

    def carried_states(half, at_pair):
        pair = (2 * at_pair, 2 * at_pair + 1)
        set_drive(pair)
        for n, _, i, wb in each_state(two_rows(at_pair), writes, half * HALF, half * HALF + HALF):
            r2 = rates[n]
            l = [jnp.zeros((S, D), F32)] * 2
            for k in range(K):
                v = leave_v[half, k, i]
                for u, h in enumerate(pair):
                    e = jnp.exp2(steps[h, k] * r2)
                    v = e * v + drive[u, k] * wb[u][k]
                    l[u] = e * l[u] + v
                leave_v[half, k, i] = v
            for u, h in enumerate(pair):
                products[u, S * n : S * n + S, :] = jnp.exp2(-r2 * upto[h]) * l[u]
        for u, h in enumerate(pair):
            passed = jnp.zeros((HALF, D), F32)
            for g in range(S):
                earlier[h, half, HALF * g : HALF * g + HALF, :] = passed
                passed = passed + products[u, pl.ds(S * HALF * half + g, HALF, stride=S), :]
            leave_s[h, half] = jnp.exp2(slow[states_of(half), :] * sum_cols[h]) * passed

    def enter(joined, h, half, entering):
        for g in range(S):
            at_g = slice(HALF * g, HALF * g + HALF)
            joined[h, half, at_g, :] = joined[h, half, at_g, :] + entering

    def carried_adjoint(half, i):
        at_pair = mid - 1 - i
        pair = (2 * at_pair, 2 * at_pair + 1)
        for h in pair:
            enter(later, h, half,
                  jnp.exp2(slow[states_of(half), :] * sum_cols[h]) * from_right[h, half])
        for n, _, i, rb in each_state(two_rows(at_pair), reads, half * HALF, half * HALF + HALF):
            r2 = rates[n]
            a = [jnp.exp2(-r2 * upto[h]) * later[h, half, pl.ds(i, S, stride=HALF), :]
                 for h in pair]
            for k in reversed(range(K)):
                p = leave_p[half, k, i]
                for u in (1, 0):
                    h = pair[u]
                    e = jnp.exp2(steps[h, k] * r2)
                    ah = a[u] + rb[u][k] * grads[h, k]
                    p = e * (ah + p)
                    a[u] = e * ah
                leave_p[half, k, i] = p

    def store_sums(out, at_pair, sums):
        out[2 * at_pair] = sums[:, :cols]
        out[2 * at_pair + 1] = sums[:, cols:]

    def final_states(at_pair):
        pair = (2 * at_pair, 2 * at_pair + 1)
        for h in pair:
            for half in range(2):
                enter(earlier, h, half, from_left[h, half])
        set_drive(pair)
        sums = jnp.zeros((NS, 2 * cols), F32)
        for n, half, i, wb in each_state(two_rows(at_pair), writes, 0, NS):
            sums = sums + channel_sums(products[n], picker, n)
            r2 = rates[n]
            s = [jnp.exp2(r2 * before[h]) * earlier[h, half, pl.ds(i, S, stride=HALF), :]
                 for h in pair]
            for k in range(K):
                v = from_above[half, k, i]
                for u, h in enumerate(pair):
                    e = jnp.exp2(steps[h, k] * r2)
                    q = e * v
                    v = q + drive[u, k] * wb[u][k]
                    t = e * s[u]
                    s[u] = t + v
                    kept_v[h, k, n] = q
                    kept_s[h, k, n] = t
                    products[n, pl.ds(cols * u + k, S, stride=K), :] = s[u] * grads[h, k]
                from_above[half, k, i] = v
        store_sums(g_read, jnp.maximum(at_pair - 1, 0), sums)

    def final_adjoint(i):
        at_pair = mid - 1 - i
        pair = (2 * at_pair, 2 * at_pair + 1)
        codes = two_rows(at_pair)
        set_drive(pair)
        through = [[jnp.zeros((S, D), F32)] * K for _ in range(2)]
        rated = [[jnp.zeros((S, D), F32)] * K for _ in range(2)]
        sums = jnp.zeros((NS, 2 * cols), F32)
        for n in range(NS):
            half, i = divmod(n, HALF)
            spreads = spread(codes, both, n)
            sums = sums + channel_sums(products[n], picker, n)
            r2 = rates[n]
            a = [jnp.exp2(-r2 * upto[h]) * later[h, half, pl.ds(i, S, stride=HALF), :]
                 for h in pair]
            stepped = jnp.zeros((S, D), F32)
            for k in reversed(range(K)):
                b = from_below[half, k, i]
                for u in (1, 0):
                    h = pair[u]
                    dt = steps[h, k]
                    e = jnp.exp2(dt * r2)
                    ah = a[u] + tile_of(spreads, cols * u + S * k, 1) * grads[h, k]
                    av = ah + b
                    b = e * av
                    a[u] = e * ah
                    eg = ah * kept_s[h, k, n] + av * kept_v[h, k, n]
                    through[u][k] = through[u][k] + av * tile_of(spreads, cols * u + S * k, 0)
                    rated[u][k] = rated[u][k] + eg * r2
                    stepped = stepped + eg * dt
                    products[n, pl.ds(cols * u + k, S, stride=K), :] = av * drive[u, k]
                from_below[half, k, i] = b
            part[n] += stepped
        store_sums(g_write, jnp.minimum(at_pair + 1, mid - 1), sums)
        for u, h in enumerate(pair):
            for k in range(K):
                g_feat[h, pl.ds(k, S, stride=K), :] = steps[h, k] * through[u][k]
                g_step[h, pl.ds(k, S, stride=K), :] = (
                    column(feat, h, k, K) * through[u][k] + LN2 * rated[u][k])

    def last_sums():
        sums = jnp.zeros((NS, 2 * cols), F32)
        for n in range(NS):
            sums = sums + channel_sums(products[n], picker, n)
        return sums

    def send(src, dst, sems, kind, o, peer):
        copy = pltpu.make_async_remote_copy(
            src_ref=src, dst_ref=dst, send_sem=sems.at[kind, o], recv_sem=sems.at[kind + 1, o],
            device_id=peer, device_id_type=MESH)
        copy.start()
        return copy

    def arrive(copies):
        for copy in copies:
            copy.wait()

    mine_k, mine_h = pl.ds(ri * kr, kr), pl.ds(ci * hc, hc)

    def scatter_rows(source, box, kind):
        box(ri)[...] = source(mine_k)[...]
        return [send(source(pl.ds(p[0] * kr, kr)), box(ri), row_sems, kind, o, p)
                for o, p in enumerate(row_peers)]

    def scatter_cols(source, box, kind):
        box[ci] = source(mine_h)[...]
        return [send(source(pl.ds(p[1] * hc, hc)), box.at[ci], col_sems, kind, o, p)
                for o, p in enumerate(col_peers)]

    def return_rows(box, target, kind):
        target(mine_k)[...] = box(ri)[...]
        return [send(box(p[0]), target(mine_k), row_sems, kind, o, p)
                for o, p in enumerate(row_peers)]

    def return_cols(box, target, kind):
        target(mine_h)[...] = box[ci]
        return [send(box.at[p[1]], target(mine_h), col_sems, kind, o, p)
                for o, p in enumerate(col_peers)]

    def scan_cols(source, result, backward):
        for half in range(2):
            rate = slow[states_of(half), :]
            for j in range(hc):
                now = jnp.zeros((HALF, D), F32)
                for c in (reversed(range(nc)) if backward else range(nc)):
                    result[c, j, half] = now
                    now = jnp.exp2(rate * sums_c[c, j]) * now + source[c, j, half]

    lax.fori_loop(0, rows, code, 0, unroll=4)
    part_way = mid // 2

    def scan_rows(half, backward):
        def one(i, carry):
            r2 = rates[half * HALF + i]
            for j in range(kr):
                now = jnp.zeros((S, D), F32)
                for r in (reversed(range(nr)) if backward else range(nr)):
                    out_r[r, half, j, i] = now
                    now = jnp.exp2(r2 * sums_r[r, j]) * now + in_r[r, half, j, i]
            return carry

        lax.fori_loop(0, HALF, one, 0)

    def rows_out(half, leave, kind):
        return scatter_rows(lambda k: leave.at[half, k], lambda r: in_r.at[r, half], kind)

    def rows_back(half, flight, backward, target, kind):
        arrive(flight)
        scan_rows(half, backward)
        return return_rows(lambda r: out_r.at[r, half], lambda k: target.at[half, k], kind)

    over(0, mid, functools.partial(local_vertical, 0))
    pl.semaphore_wait(barrier, len(row_peers) + len(col_peers))
    down = [None, None]
    down[0] = rows_out(0, leave_v, 0)
    down[0] += scatter_rows(lambda k: sum_rows.at[k], lambda r: sums_r.at[r], 8)
    totals = scatter_cols(lambda h: sum_cols.at[h], sums_c, 4)
    over(0, mid, functools.partial(local_vertical, 1))
    down[1] = rows_out(1, leave_v, 4)
    fetch.wait()
    over(0, part_way, local_adjoint)
    down[0] = rows_back(0, down[0], False, from_above, 2)
    over(part_way, mid, local_adjoint)
    right = scatter_cols(lambda h: leave_a.at[h], in_c, 0)
    down[1] = rows_back(1, down[1], False, from_above, 6)
    arrive(down[0])
    leave_v[0] = from_above[0]
    over(0, mid, functools.partial(carried_states, 0))
    arrive(totals)
    arrive(right)
    scan_cols(in_c, out_c, True)
    right = return_cols(out_c, lambda h: from_right.at[h], 2)
    arrive(down[1])
    leave_v[1] = from_above[1]
    over(0, mid, functools.partial(carried_states, 1))
    arrive(right)
    left = scatter_cols(lambda h: leave_s.at[h], in_c, 6)
    over(0, mid, functools.partial(carried_adjoint, 0))
    up = [None, None]
    up[0] = rows_out(0, leave_p, 10)
    arrive(left)
    scan_cols(in_c, out_c, False)
    left = return_cols(out_c, lambda h: from_left.at[h], 8)
    over(0, mid, functools.partial(carried_adjoint, 1))
    up[1] = rows_out(1, leave_p, 14)
    arrive(left)
    over(0, part_way, final_states)
    up[0] = rows_back(0, up[0], True, from_below, 12)
    up[1] = rows_back(1, up[1], True, from_below, 16)
    over(part_way, mid, final_states)
    store_sums(g_read, mid - 1, last_sums())
    arrive(up[0])
    arrive(up[1])
    over(0, mid, final_adjoint)

    by_row[ri] = jnp.sum(part[...], axis=1)
    arrive([send(by_row.at[ri], by_row.at[ri], row_sems, 18, o, p)
            for o, p in enumerate(row_peers)])
    by_col[ci] = jnp.sum(by_row[...], axis=0)
    flight = [send(by_col.at[ci], by_col.at[ci], col_sems, 10, o, p)
              for o, p in enumerate(col_peers)]
    store_sums(g_write, 0, last_sums())
    arrive(flight)
    g_decay[...] = jnp.sum(by_col[...], axis=0) * -jnp.exp(decay_log[...])


def shards(features, step_size, write_weights, read_weights, decay_log, out_grad):
    rows, cols = step_size.shape[0], step_size.shape[1]
    K = cols // S
    nr, nc = lax.axis_size("row"), lax.axis_size("col")
    kr, hc = K // nr, rows // nc

    def vm(*shape, kind=F32):
        return pltpu.VMEM(shape, kind)

    carry_r, carry_c = vm(2, K, HALF, S, D), vm(rows, 2, HALF, D)
    grid, kept = vm(rows, K, S, D), vm(rows, K, NS, S, D)
    joined = vm(rows, 2, S * HALF, D)
    box_r = vm(nr, 2, kr, HALF, S, D)
    table = vm(6 * NS, NS * D, kind=BF16)
    box_c = vm(nc, hc, 2, HALF, D)
    args = (features, step_size, write_weights.transpose(0, 2, 1),
            read_weights.transpose(0, 2, 1), out_grad, decay_log)
    outs = [(rows, cols, D), (rows, cols, D), (rows, NS, cols), (rows, NS, cols), (NS, D)]
    g_feat, g_step, g_write, g_read, g_decay = pl.pallas_call(
        functools.partial(scan_kernel, nr, nc),
        out_shape=[jax.ShapeDtypeStruct(o, F32) for o in outs],
        in_specs=[VMEM] * 4 + [pl.BlockSpec(memory_space=pl.ANY), VMEM],
        out_specs=[VMEM] * len(outs),
        scratch_shapes=[
            vm(NS, S, D), vm(NS, D), table, table, vm(6 * NS, 2 * NS * D, kind=BF16),
            vm(NS, NS, 2 * D, kind=BF16), vm(rows * cols, 6 * NS, kind=BF16), grid, grid, vm(2, K, S, D),
            vm(rows, S, D), vm(rows, S, D), vm(rows, 1, D), vm(K, S, D), joined, joined,
            carry_r, carry_r, carry_r, carry_r,
            carry_c, carry_c, carry_c, carry_c, kept, kept,
            vm(NS, 2 * cols, D), vm(NS, S, D),
            vm(nr, kr, S, D), vm(nc, hc, 1, D), box_r, box_r, box_c, box_c, vm(nr, NS, D), vm(nc, NS, D), vm(rows, cols, D),
            pltpu.SemaphoreType.DMA((20, nr - 1)), pltpu.SemaphoreType.DMA((12, nc - 1)),
            pltpu.SemaphoreType.DMA],
        compiler_params=pltpu.CompilerParams(
            collective_id=0, has_side_effects=True, vmem_limit_bytes=48 << 20),
        name="scan",
    )(*args)
    return (g_feat, g_step, g_write.transpose(0, 2, 1), g_read.transpose(0, 2, 1), g_decay)


def solution(mesh):
    tiles = P("row", "col", None)
    in_specs = (tiles, tiles, tiles, tiles, P(), tiles)
    out_specs = (tiles, tiles, tiles, tiles, P())
    return jax.shard_map(shards, mesh=mesh, in_specs=in_specs, out_specs=out_specs, check_vma=False)
```

```python
import functools
import math
import jax
import jax.numpy as jnp
from jax import lax
from jax.experimental import pallas as pl
from jax.experimental.pallas import tpu as pltpu
from jax.sharding import PartitionSpec as P

NS = 16
HALF = 8
D = 128
S = 8
F32 = jnp.float32
BF16 = jnp.bfloat16
LOG2E = math.log2(math.e)
LN2 = math.log(2.0)
MESH = pl.DeviceIdType.MESH
VMEM = pl.BlockSpec(memory_space=pltpu.VMEM)


def column(ref, h, k, width):
    return ref[h, pl.ds(k, S, stride=width), :]


def set_rates(decay_log, rates):
    for n in range(NS):
        rates[n] = jnp.broadcast_to(-jnp.exp(decay_log[n : n + 1, :]) * LOG2E, (S, D))


def equal(a, b):
    return jnp.where(a == b, 1.0, 0.0).astype(BF16)


def set_spreaders(writes, reads, both):
    for table, parts in ((writes, (0,)), (reads, (1,)), (both, (0, 1))):
        row = lax.broadcasted_iota(jnp.int32, table.shape, 0)
        to = lax.broadcasted_iota(jnp.int32, table.shape, 1) // D
        if len(parts) == 1:
            meets = jnp.where(row // (3 * NS) == parts[0], row % NS, NS) == to
        else:
            meets = 2 * (row % NS) + row // (3 * NS) == to
        table[...] = jnp.where(meets, 1.0, 0.0).astype(BF16)


def by_segment(cols):
    K = cols // S
    at = lax.broadcasted_iota(jnp.int32, (cols, cols), 0)
    col = lax.broadcasted_iota(jnp.int32, (cols, cols), 1)
    return equal(col, (at % S) * K + at // S)


def split3(x, axis):
    high = x.astype(BF16)
    rest = x - high.astype(F32)
    mid = rest.astype(BF16)
    low = (rest - mid.astype(F32)).astype(BF16)
    return jnp.concatenate([high, mid, low], axis=axis)


def spread(coded, table, at):
    return jnp.dot(coded, table[:, 2 * D * at : 2 * D * at + 2 * D],
                   preferred_element_type=F32)


def sublane():
    return lax.broadcasted_iota(jnp.int32, (S, D), 0)


def sums_down(value, at):
    for shift in (1, 2, 4):
        value = value + jnp.where(at >= shift, pltpu.roll(value, shift, 0), 0.0)
    return value


def tile_of(block, row, half):
    return block[row : row + S, D * half : D * half + D]


def states_of(half):
    return slice(half * HALF, half * HALF + HALF)


def channel_sums(values, picker, n):
    high = values.astype(BF16)
    low = (values - high.astype(F32)).astype(BF16)
    return lax.dot_general(
        picker[n], jnp.concatenate([high, low], axis=1), (((1,), (1,)), ((), ())),
        preferred_element_type=F32)


def scan_kernel(nr, nc, feat_far, step_far, write_far, read_far, grad_far, decay_log,
                g_feat, g_step, g_write, g_read, g_decay,
                rates, slow, writes, reads, both, picker, coded, steps, grads, drive,
                before, upto, sum_cols, later, earlier,
                leave_v, leave_p, from_above, from_below,
                leave_a, leave_s, from_right, from_left, kept_s, kept_v, products, part,
                in_r, out_r, in_c, out_c,
                by_row, by_col, write, read, step, feat,
                row_sems, col_sems, fetch_sems):
    rows, cols = step_far.shape[0], step_far.shape[1]
    K = cols // S
    mid = rows // 2
    ri, ci = lax.axis_index("row"), lax.axis_index("col")
    kr, hc = K // nr, rows // nc
    row_peers = [(lax.rem(ri + o, nr), ci) for o in range(1, nr)]
    col_peers = [(ri, lax.rem(ci + o, nc)) for o in range(1, nc)]
    fetches = [
        pltpu.make_async_copy(far, near, fetch_sems.at[i])
        for i, (far, near) in enumerate((
            (write_far, write), (read_far, read), (step_far, step), (feat_far, feat),
            (grad_far, products)))]
    for fetch in fetches:
        fetch.start()
    barrier = pltpu.get_barrier_semaphore()
    for peer in row_peers + col_peers:
        pl.semaphore_signal(barrier, inc=1, device_id=peer, device_id_type=MESH)

    set_rates(decay_log, rates)
    set_spreaders(writes, reads, both)
    slow[...] = -jnp.exp(decay_log[...]) * LOG2E
    picked = lax.broadcasted_iota(jnp.int32, picker.shape[1:], 0)
    for n in range(NS):
        picker[n] = equal(picked, n)
    leave_v[...] = jnp.zeros_like(leave_v)
    leave_p[...] = jnp.zeros_like(leave_p)
    part[...] = jnp.zeros_like(part)
    at = sublane()
    turn = by_segment(cols)

    def code(h, carry):
        parts = jnp.concatenate([split3(write[h], 0), split3(read[h], 0)], axis=0)
        coded[pl.ds(pl.multiple_of(h * cols, cols), cols), :] = lax.dot_general(
            turn, parts, (((1,), (1,)), ((), ())), preferred_element_type=F32).astype(BF16)
        return carry

    def two_rows(i):
        return coded[pl.ds(pl.multiple_of(2 * cols * i, 2 * cols), 2 * cols), :]

    def set_drive(pair):
        for u, h in enumerate(pair):
            for k in range(K):
                drive[u, k] = steps[h, k] * column(feat, h, k, K)

    def each_state(codes, table, lo, hi):
        for pair in range(lo // 2, hi // 2):
            spreads = spread(codes, table, pair)
            for j in range(2):
                n = 2 * pair + j
                half, i = divmod(n, HALF)
                yield n, half, i, [
                    [tile_of(spreads, cols * u + S * k, j) for k in range(K)] for u in range(2)]

    def over(lo, hi, row):
        def one(i, carry):
            row(i)
            return carry

        lax.fori_loop(lo, hi, one, 0)

    def local_vertical(half, at_pair):
        pair = (2 * at_pair, 2 * at_pair + 1)
        if half == 0:
            for h in pair:
                total = jnp.zeros((S, D), F32)
                for k in range(K):
                    dt = column(step, h, k, K)
                    steps[h, k] = dt
                    total = total + dt
                    leave_v[0, k, HALF] += dt
                ends = sums_down(total, at)
                upto[h] = ends
                before[h] = ends - total
                sum_cols[h] = ends[S - 1 :, :]
                leave_a[h, 2] = jnp.broadcast_to(ends[S - 1 :, :], (HALF, D))
        set_drive(pair)
        for n, _, i, wb in each_state(two_rows(at_pair), writes, half * HALF, half * HALF + HALF):
            r2 = rates[n]
            for k in range(K):
                v = leave_v[half, k, i]
                for u, h in enumerate(pair):
                    v = jnp.exp2(steps[h, k] * r2) * v + drive[u, k] * wb[u][k]
                leave_v[half, k, i] = v

    def set_grads(at_pair):
        for u in range(2):
            for k in range(K):
                grads[2 * at_pair + u, k] = products[at_pair, pl.ds(cols * u + k, S, stride=K), :]

    def local_adjoint(at_pair):
        pair = (2 * at_pair, 2 * at_pair + 1)
        for n, _, _, rb in each_state(two_rows(at_pair), reads, 0, NS):
            r2 = rates[n]
            for u, h in enumerate(pair):
                a = jnp.zeros((S, D), F32)
                for k in reversed(range(K)):
                    a = jnp.exp2(steps[h, k] * r2) * (a + rb[u][k] * grads[h, k])
                products[u, S * n : S * n + S, :] = jnp.exp2(r2 * before[h]) * a
        for u, h in enumerate(pair):
            for half in range(2):
                passed = jnp.zeros((HALF, D), F32)
                for g in reversed(range(S)):
                    later[h, half, HALF * g : HALF * g + HALF, :] = passed
                    passed = passed + products[u, pl.ds(S * HALF * half + g, HALF, stride=S), :]
                leave_a[h, half] = passed

    def carried_states(half, at_pair):
        pair = (2 * at_pair, 2 * at_pair + 1)
        set_drive(pair)
        for n, _, i, wb in each_state(two_rows(at_pair), writes, half * HALF, half * HALF + HALF):
            r2 = rates[n]
            l = [jnp.zeros((S, D), F32)] * 2
            for k in range(K):
                v = leave_v[half, k, i]
                for u, h in enumerate(pair):
                    e = jnp.exp2(steps[h, k] * r2)
                    v = e * v + drive[u, k] * wb[u][k]
                    l[u] = e * l[u] + v
                leave_v[half, k, i] = v
            for u, h in enumerate(pair):
                products[u, S * n : S * n + S, :] = jnp.exp2(-r2 * upto[h]) * l[u]
        for u, h in enumerate(pair):
            passed = jnp.zeros((HALF, D), F32)
            for g in range(S):
                earlier[h, half, HALF * g : HALF * g + HALF, :] = passed
                passed = passed + products[u, pl.ds(S * HALF * half + g, HALF, stride=S), :]
            leave_s[h, half] = jnp.exp2(slow[states_of(half), :] * sum_cols[h]) * passed

    def enter(joined, h, half, entering):
        for g in range(S):
            at_g = slice(HALF * g, HALF * g + HALF)
            joined[h, half, at_g, :] = joined[h, half, at_g, :] + entering

    def carried_adjoint(half, i):
        at_pair = mid - 1 - i
        pair = (2 * at_pair, 2 * at_pair + 1)
        for h in pair:
            enter(later, h, half,
                  jnp.exp2(slow[states_of(half), :] * sum_cols[h]) * from_right[h, half])
        for n, _, i, rb in each_state(two_rows(at_pair), reads, half * HALF, half * HALF + HALF):
            r2 = rates[n]
            a = [jnp.exp2(-r2 * upto[h]) * later[h, half, pl.ds(i, S, stride=HALF), :]
                 for h in pair]
            for k in reversed(range(K)):
                p = leave_p[half, k, i]
                for u in (1, 0):
                    h = pair[u]
                    e = jnp.exp2(steps[h, k] * r2)
                    ah = a[u] + rb[u][k] * grads[h, k]
                    p = e * (ah + p)
                    a[u] = e * ah
                leave_p[half, k, i] = p

    def store_sums(out, at_pair, sums):
        out[2 * at_pair] = sums[:, :cols]
        out[2 * at_pair + 1] = sums[:, cols:]

    def final_states(at_pair):
        pair = (2 * at_pair, 2 * at_pair + 1)
        for h in pair:
            for half in range(2):
                enter(earlier, h, half, from_left[h, half])
        set_drive(pair)
        sums = jnp.zeros((NS, 2 * cols), F32)
        for n, half, i, wb in each_state(two_rows(at_pair), writes, 0, NS):
            sums = sums + channel_sums(products[n], picker, n)
            r2 = rates[n]
            s = [jnp.exp2(r2 * before[h]) * earlier[h, half, pl.ds(i, S, stride=HALF), :]
                 for h in pair]
            for k in range(K):
                v = from_above[half, k, i]
                for u, h in enumerate(pair):
                    e = jnp.exp2(steps[h, k] * r2)
                    q = e * v
                    v = q + drive[u, k] * wb[u][k]
                    t = e * s[u]
                    s[u] = t + v
                    kept_v[h, k, n] = q
                    kept_s[h, k, n] = t
                    products[n, pl.ds(cols * u + k, S, stride=K), :] = s[u] * grads[h, k]
                from_above[half, k, i] = v
        store_sums(g_read, jnp.maximum(at_pair - 1, 0), sums)

    def final_adjoint(i):
        at_pair = mid - 1 - i
        pair = (2 * at_pair, 2 * at_pair + 1)
        codes = two_rows(at_pair)
        set_drive(pair)
        through = [[jnp.zeros((S, D), F32)] * K for _ in range(2)]
        rated = [[jnp.zeros((S, D), F32)] * K for _ in range(2)]
        sums = jnp.zeros((NS, 2 * cols), F32)
        for n in range(NS):
            half, i = divmod(n, HALF)
            spreads = spread(codes, both, n)
            sums = sums + channel_sums(products[n], picker, n)
            r2 = rates[n]
            a = [jnp.exp2(-r2 * upto[h]) * later[h, half, pl.ds(i, S, stride=HALF), :]
                 for h in pair]
            stepped = jnp.zeros((S, D), F32)
            for k in reversed(range(K)):
                b = from_below[half, k, i]
                for u in (1, 0):
                    h = pair[u]
                    dt = steps[h, k]
                    e = jnp.exp2(dt * r2)
                    ah = a[u] + tile_of(spreads, cols * u + S * k, 1) * grads[h, k]
                    av = ah + b
                    b = e * av
                    a[u] = e * ah
                    eg = ah * kept_s[h, k, n] + av * kept_v[h, k, n]
                    through[u][k] = through[u][k] + av * tile_of(spreads, cols * u + S * k, 0)
                    rated[u][k] = rated[u][k] + eg * r2
                    stepped = stepped + eg * dt
                    products[n, pl.ds(cols * u + k, S, stride=K), :] = av * drive[u, k]
                from_below[half, k, i] = b
            part[n] += stepped
        store_sums(g_write, jnp.minimum(at_pair + 1, mid - 1), sums)
        for u, h in enumerate(pair):
            for k in range(K):
                g_feat[h, pl.ds(k, S, stride=K), :] = steps[h, k] * through[u][k]
                g_step[h, pl.ds(k, S, stride=K), :] = (
                    column(feat, h, k, K) * through[u][k] + LN2 * rated[u][k])

    def last_sums():
        sums = jnp.zeros((NS, 2 * cols), F32)
        for n in range(NS):
            sums = sums + channel_sums(products[n], picker, n)
        return sums

    def send(src, dst, sems, kind, o, peer):
        copy = pltpu.make_async_remote_copy(
            src_ref=src, dst_ref=dst, send_sem=sems.at[kind, o], recv_sem=sems.at[kind + 1, o],
            device_id=peer, device_id_type=MESH)
        copy.start()
        return copy

    def arrive(copies):
        for copy in copies:
            copy.wait()

    mine_k, mine_h = pl.ds(ri * kr, kr), pl.ds(ci * hc, hc)

    def scatter_rows(source, box, kind):
        box(ri)[...] = source(mine_k)[...]
        return [send(source(pl.ds(p[0] * kr, kr)), box(ri), row_sems, kind, o, p)
                for o, p in enumerate(row_peers)]

    def scatter_cols(source, box, kind):
        box(ci)[...] = source(mine_h)[...]
        return [send(source(pl.ds(p[1] * hc, hc)), box(ci), col_sems, kind, o, p)
                for o, p in enumerate(col_peers)]

    def return_rows(box, target, kind):
        target(mine_k)[...] = box(ri)[...]
        return [send(box(p[0]), target(mine_k), row_sems, kind, o, p)
                for o, p in enumerate(row_peers)]

    def return_cols(box, target, kind):
        target(mine_h)[...] = box[ci]
        return [send(box.at[p[1]], target(mine_h), col_sems, kind, o, p)
                for o, p in enumerate(col_peers)]

    def scan_cols(source, result, backward):
        for half in range(2):
            rate = slow[states_of(half), :]
            for j in range(hc):
                now = jnp.zeros((HALF, D), F32)
                for c in (reversed(range(nc)) if backward else range(nc)):
                    result[c, j, half] = now
                    now = jnp.exp2(rate * source[c, j, 2]) * now + source[c, j, half]

    fetches[0].wait()
    fetches[1].wait()
    lax.fori_loop(0, rows, code, 0, unroll=4)
    fetches[2].wait()
    fetches[3].wait()
    part_way = mid // 2

    def scan_rows(half, backward):
        def one(i, carry):
            r2 = rates[half * HALF + i]
            for j in range(kr):
                now = jnp.zeros((S, D), F32)
                for r in (reversed(range(nr)) if backward else range(nr)):
                    out_r[r, half, j, i] = now
                    now = jnp.exp2(r2 * in_r[r, 0, j, HALF]) * now + in_r[r, half, j, i]
            return carry

        lax.fori_loop(0, HALF, one, 0)

    def rows_out(half, leave, kind, width=HALF):
        part_of = pl.ds(0, width)
        return scatter_rows(lambda k: leave.at[half, k, part_of],
                            lambda r: in_r.at[r, half, :, part_of], kind)

    def rows_back(half, flight, backward, target, kind):
        arrive(flight)
        scan_rows(half, backward)
        return return_rows(lambda r: out_r.at[r, half], lambda k: target.at[half, k], kind)

    over(0, mid, functools.partial(local_vertical, 0))
    pl.semaphore_wait(barrier, len(row_peers) + len(col_peers))
    down = [None, None]
    down[0] = rows_out(0, leave_v, 0, HALF + 1)
    over(0, mid, functools.partial(local_vertical, 1))
    down[1] = rows_out(1, leave_v, 4)
    fetches[4].wait()
    over(0, mid, set_grads)
    over(0, part_way, local_adjoint)
    down[0] = rows_back(0, down[0], False, from_above, 2)
    over(part_way, mid, local_adjoint)
    right = scatter_cols(lambda h: leave_a.at[h], lambda c: in_c.at[c], 0)
    down[1] = rows_back(1, down[1], False, from_above, 6)
    arrive(down[0])
    leave_v[0, :, :HALF] = from_above[0]
    over(0, mid, functools.partial(carried_states, 0))
    arrive(right)
    scan_cols(in_c, out_c, True)
    right = return_cols(out_c, lambda h: from_right.at[h], 2)
    arrive(down[1])
    leave_v[1, :, :HALF] = from_above[1]
    over(0, mid, functools.partial(carried_states, 1))
    arrive(right)
    left = scatter_cols(lambda h: leave_s.at[h], lambda c: in_c.at[c, :, pl.ds(0, 2)], 6)
    over(0, mid, functools.partial(carried_adjoint, 0))
    up = [None, None]
    up[0] = rows_out(0, leave_p, 10)
    arrive(left)
    scan_cols(in_c, out_c, False)
    left = return_cols(out_c, lambda h: from_left.at[h], 8)
    over(0, mid, functools.partial(carried_adjoint, 1))
    up[1] = rows_out(1, leave_p, 14)
    arrive(left)
    over(0, part_way, final_states)
    up[0] = rows_back(0, up[0], True, from_below, 12)
    up[1] = rows_back(1, up[1], True, from_below, 16)
    over(part_way, mid, final_states)
    store_sums(g_read, mid - 1, last_sums())
    arrive(up[0])
    arrive(up[1])
    over(0, mid, final_adjoint)

    by_row[ri] = jnp.sum(part[...], axis=1)
    arrive([send(by_row.at[ri], by_row.at[ri], row_sems, 18, o, p)
            for o, p in enumerate(row_peers)])
    by_col[ci] = jnp.sum(by_row[...], axis=0)
    flight = [send(by_col.at[ci], by_col.at[ci], col_sems, 10, o, p)
              for o, p in enumerate(col_peers)]
    store_sums(g_write, 0, last_sums())
    arrive(flight)
    g_decay[...] = jnp.sum(by_col[...], axis=0) * -jnp.exp(decay_log[...])


def shards(features, step_size, write_weights, read_weights, decay_log, out_grad):
    rows, cols = step_size.shape[0], step_size.shape[1]
    K = cols // S
    nr, nc = lax.axis_size("row"), lax.axis_size("col")
    kr, hc = K // nr, rows // nc

    def vm(*shape, kind=F32):
        return pltpu.VMEM(shape, kind)

    carry_r, carry_c = vm(2, K, HALF, S, D), vm(rows, 2, HALF, D)
    grid, kept = vm(rows, K, S, D), vm(rows, K, NS, S, D)
    joined = vm(rows, 2, S * HALF, D)
    raw = vm(rows, cols, D)
    box_r = vm(nr, 2, kr, HALF, S, D)
    table = vm(6 * NS, NS * D, kind=BF16)
    box_c = vm(nc, hc, 2, HALF, D)
    args = (features, step_size, write_weights.transpose(0, 2, 1),
            read_weights.transpose(0, 2, 1), out_grad.reshape(NS, 2 * cols, D), decay_log)
    outs = [(rows, cols, D), (rows, cols, D), (rows, NS, cols), (rows, NS, cols), (NS, D)]
    g_feat, g_step, g_write, g_read, g_decay = pl.pallas_call(
        functools.partial(scan_kernel, nr, nc),
        out_shape=[jax.ShapeDtypeStruct(o, F32) for o in outs],
        in_specs=[pl.BlockSpec(memory_space=pl.ANY)] * 5 + [VMEM],
        out_specs=[VMEM] * len(outs),
        scratch_shapes=[
            vm(NS, S, D), vm(NS, D), table, table, vm(6 * NS, 2 * NS * D, kind=BF16),
            vm(NS, NS, 2 * D, kind=BF16), vm(rows * cols, 6 * NS, kind=BF16), grid, grid, vm(2, K, S, D),
            vm(rows, S, D), vm(rows, S, D), vm(rows, 1, D), joined, joined,
            vm(2, K, HALF + 1, S, D), carry_r, carry_r, carry_r,
            vm(rows, 3, HALF, D), carry_c, carry_c, carry_c, kept, kept,
            vm(NS, 2 * cols, D), vm(NS, S, D),
            vm(nr, 2, kr, HALF + 1, S, D), box_r, vm(nc, hc, 3, HALF, D), box_c, vm(nr, NS, D), vm(nc, NS, D),
            vm(rows, NS, cols), vm(rows, NS, cols), raw, raw,
            pltpu.SemaphoreType.DMA((20, nr - 1)), pltpu.SemaphoreType.DMA((12, nc - 1)),
            pltpu.SemaphoreType.DMA((5,))],
        compiler_params=pltpu.CompilerParams(
            collective_id=0, has_side_effects=True, vmem_limit_bytes=50 << 20),
        name="scan",
    )(*args)
    return (g_feat, g_step, g_write.transpose(0, 2, 1), g_read.transpose(0, 2, 1), g_decay)


def solution(mesh):
    tiles = P("row", "col", None)
    in_specs = (tiles, tiles, tiles, tiles, P(), tiles)
    out_specs = (tiles, tiles, tiles, tiles, P())
    return jax.shard_map(shards, mesh=mesh, in_specs=in_specs, out_specs=out_specs, check_vma=False)
```

```python
import functools
import math
import jax
import jax.numpy as jnp
from jax import lax
from jax.experimental import pallas as pl
from jax.experimental.pallas import tpu as pltpu
from jax.sharding import PartitionSpec as P

NS = 16
HALF = 8
D = 128
S = 8
F32 = jnp.float32
BF16 = jnp.bfloat16
LOG2E = math.log2(math.e)
LN2 = math.log(2.0)
MESH = pl.DeviceIdType.MESH
VMEM = pl.BlockSpec(memory_space=pltpu.VMEM)


def column(ref, h, k, width):
    return ref[h, pl.ds(k, S, stride=width), :]


def set_rates(decay_log, rates):
    for n in range(NS):
        rates[n] = jnp.broadcast_to(-jnp.exp(decay_log[n : n + 1, :]) * LOG2E, (S, D))


def equal(a, b):
    return jnp.where(a == b, 1.0, 0.0).astype(BF16)


def set_spreaders(writes, reads, both):
    for table, parts in ((writes, (0,)), (reads, (1,)), (both, (0, 1))):
        row = lax.broadcasted_iota(jnp.int32, table.shape, 0)
        to = lax.broadcasted_iota(jnp.int32, table.shape, 1) // D
        if len(parts) == 1:
            meets = jnp.where(row // (3 * NS) == parts[0], row % NS, NS) == to
        else:
            meets = 2 * (row % NS) + row // (3 * NS) == to
        table[...] = jnp.where(meets, 1.0, 0.0).astype(BF16)


def by_segment(cols):
    K = cols // S
    at = lax.broadcasted_iota(jnp.int32, (cols, cols), 0)
    col = lax.broadcasted_iota(jnp.int32, (cols, cols), 1)
    return equal(col, (at % S) * K + at // S)


def split3(x, axis):
    high = x.astype(BF16)
    rest = x - high.astype(F32)
    mid = rest.astype(BF16)
    low = (rest - mid.astype(F32)).astype(BF16)
    return jnp.concatenate([high, mid, low], axis=axis)


def spread(coded, table, at):
    return jnp.dot(coded, table[:, 2 * D * at : 2 * D * at + 2 * D],
                   preferred_element_type=F32)


def sublane():
    return lax.broadcasted_iota(jnp.int32, (S, D), 0)


def sums_down(value, at):
    for shift in (1, 2, 4):
        value = value + jnp.where(at >= shift, pltpu.roll(value, shift, 0), 0.0)
    return value


def tile_of(block, row, half):
    return block[row : row + S, D * half : D * half + D]


def states_of(half):
    return slice(half * HALF, half * HALF + HALF)


def channel_sums(values, picker, n):
    high = values.astype(BF16)
    low = (values - high.astype(F32)).astype(BF16)
    return lax.dot_general(
        picker[n], jnp.concatenate([high, low], axis=1), (((1,), (1,)), ((), ())),
        preferred_element_type=F32)


def scan_kernel(nr, nc, feat_far, step_far, write_far, read_far, grad_far, decay_log,
                g_feat, g_step, g_write, g_read, g_decay,
                rates, slow, writes, reads, both, picker, coded, steps, grads, drive,
                before, upto, sum_cols, later, earlier,
                leave_v, leave_p, from_above, from_below,
                leave_a, leave_s, from_right, from_left, kept_s, kept_v, products, part,
                in_r, out_r, in_c, out_c,
                by_row, by_col, write, read, step, feat,
                row_sems, col_sems, fetch_sems):
    rows, cols = step_far.shape[0], step_far.shape[1]
    K = cols // S
    mid = rows // 2
    ri, ci = lax.axis_index("row"), lax.axis_index("col")
    kr, hc = K // nr, rows // nc
    row_peers = [(lax.rem(ri + o, nr), ci) for o in range(1, nr)]
    col_peers = [(ri, lax.rem(ci + o, nc)) for o in range(1, nc)]
    fetches = [
        pltpu.make_async_copy(far, near, fetch_sems.at[i])
        for i, (far, near) in enumerate((
            (write_far, write), (read_far, read), (step_far, step), (feat_far, feat),
            (grad_far, products)))]
    for fetch in fetches:
        fetch.start()
    barrier = pltpu.get_barrier_semaphore()
    for peer in row_peers + col_peers:
        pl.semaphore_signal(barrier, inc=1, device_id=peer, device_id_type=MESH)

    set_rates(decay_log, rates)
    set_spreaders(writes, reads, both)
    slow[...] = -jnp.exp(decay_log[...]) * LOG2E
    picked = lax.broadcasted_iota(jnp.int32, picker.shape[1:], 0)
    for n in range(NS):
        picker[n] = equal(picked, n)
    leave_v[...] = jnp.zeros_like(leave_v)
    leave_p[...] = jnp.zeros_like(leave_p)
    part[...] = jnp.zeros_like(part)
    at = sublane()
    turn = by_segment(cols)

    def code(h, carry):
        parts = jnp.concatenate([split3(write[h], 0), split3(read[h], 0)], axis=0)
        coded[pl.ds(pl.multiple_of(h * cols, cols), cols), :] = lax.dot_general(
            turn, parts, (((1,), (1,)), ((), ())), preferred_element_type=F32).astype(BF16)
        return carry

    def two_rows(i):
        return coded[pl.ds(pl.multiple_of(2 * cols * i, 2 * cols), 2 * cols), :]

    def set_drive(pair):
        for u, h in enumerate(pair):
            for k in range(K):
                drive[u, k] = steps[h, k] * column(feat, h, k, K)

    def each_state(codes, table, lo, hi):
        for pair in range(lo // 2, hi // 2):
            spreads = spread(codes, table, pair)
            for j in range(2):
                n = 2 * pair + j
                half, i = divmod(n, HALF)
                yield n, half, i, [
                    [tile_of(spreads, cols * u + S * k, j) for k in range(K)] for u in range(2)]

    def over(lo, hi, row):
        def one(i, carry):
            row(i)
            return carry

        lax.fori_loop(lo, hi, one, 0)

    def local_vertical(half, at_pair):
        pair = (2 * at_pair, 2 * at_pair + 1)
        if half == 0:
            for h in pair:
                total = jnp.zeros((S, D), F32)
                for k in range(K):
                    dt = column(step, h, k, K)
                    steps[h, k] = dt
                    total = total + dt
                    leave_v[0, k, HALF] += dt
                ends = sums_down(total, at)
                upto[h] = ends
                before[h] = ends - total
                sum_cols[h] = ends[S - 1 :, :]
                leave_a[h, 2] = jnp.broadcast_to(ends[S - 1 :, :], (HALF, D))
        set_drive(pair)
        for n, _, i, wb in each_state(two_rows(at_pair), writes, half * HALF, half * HALF + HALF):
            r2 = rates[n]
            for k in range(K):
                v = leave_v[half, k, i]
                for u, h in enumerate(pair):
                    v = jnp.exp2(steps[h, k] * r2) * v + drive[u, k] * wb[u][k]
                leave_v[half, k, i] = v

    def set_grads(at_pair):
        for u in range(2):
            for k in range(K):
                grads[2 * at_pair + u, k] = products[at_pair, pl.ds(cols * u + k, S, stride=K), :]

    def local_adjoint(at_pair):
        pair = (2 * at_pair, 2 * at_pair + 1)
        for n, _, _, rb in each_state(two_rows(at_pair), reads, 0, NS):
            r2 = rates[n]
            for u, h in enumerate(pair):
                a = jnp.zeros((S, D), F32)
                for k in reversed(range(K)):
                    a = jnp.exp2(steps[h, k] * r2) * (a + rb[u][k] * grads[h, k])
                products[u, S * n : S * n + S, :] = jnp.exp2(r2 * before[h]) * a
        for u, h in enumerate(pair):
            for half in range(2):
                passed = jnp.zeros((HALF, D), F32)
                for g in reversed(range(S)):
                    later[h, half, HALF * g : HALF * g + HALF, :] = passed
                    passed = passed + products[u, pl.ds(S * HALF * half + g, HALF, stride=S), :]
                leave_a[h, half] = passed

    def carried_states(half, at_pair):
        pair = (2 * at_pair, 2 * at_pair + 1)
        set_drive(pair)
        for n, _, i, wb in each_state(two_rows(at_pair), writes, half * HALF, half * HALF + HALF):
            r2 = rates[n]
            l = [jnp.zeros((S, D), F32)] * 2
            for k in range(K):
                v = leave_v[half, k, i]
                for u, h in enumerate(pair):
                    e = jnp.exp2(steps[h, k] * r2)
                    v = e * v + drive[u, k] * wb[u][k]
                    l[u] = e * l[u] + v
                leave_v[half, k, i] = v
            for u, h in enumerate(pair):
                products[u, S * n : S * n + S, :] = jnp.exp2(-r2 * upto[h]) * l[u]
        for u, h in enumerate(pair):
            passed = jnp.zeros((HALF, D), F32)
            for g in range(S):
                earlier[h, half, HALF * g : HALF * g + HALF, :] = passed
                passed = passed + products[u, pl.ds(S * HALF * half + g, HALF, stride=S), :]
            leave_s[h, half] = jnp.exp2(slow[states_of(half), :] * sum_cols[h]) * passed

    def enter(joined, h, half, entering):
        for g in range(S):
            at_g = slice(HALF * g, HALF * g + HALF)
            joined[h, half, at_g, :] = joined[h, half, at_g, :] + entering

    def carried_adjoint(half, i):
        at_pair = mid - 1 - i
        pair = (2 * at_pair, 2 * at_pair + 1)
        for h in pair:
            enter(later, h, half,
                  jnp.exp2(slow[states_of(half), :] * sum_cols[h]) * from_right[h, half])
        for n, _, i, rb in each_state(two_rows(at_pair), reads, half * HALF, half * HALF + HALF):
            r2 = rates[n]
            a = [jnp.exp2(-r2 * upto[h]) * later[h, half, pl.ds(i, S, stride=HALF), :]
                 for h in pair]
            for k in reversed(range(K)):
                p = leave_p[half, k, i]
                for u in (1, 0):
                    h = pair[u]
                    e = jnp.exp2(steps[h, k] * r2)
                    ah = a[u] + rb[u][k] * grads[h, k]
                    p = e * (ah + p)
                    a[u] = e * ah
                leave_p[half, k, i] = p

    def store_sums(out, at_pair, sums):
        out[2 * at_pair] = sums[:, :cols]
        out[2 * at_pair + 1] = sums[:, cols:]

    def final_states(at_pair):
        pair = (2 * at_pair, 2 * at_pair + 1)
        for h in pair:
            for half in range(2):
                enter(earlier, h, half, from_left[h, half])
        set_drive(pair)
        sums = jnp.zeros((NS, 2 * cols), F32)
        for n, half, i, wb in each_state(two_rows(at_pair), writes, 0, NS):
            sums = sums + channel_sums(products[n], picker, n)
            r2 = rates[n]
            s = [jnp.exp2(r2 * before[h]) * earlier[h, half, pl.ds(i, S, stride=HALF), :]
                 for h in pair]
            for k in range(K):
                v = from_above[half, k, i]
                for u, h in enumerate(pair):
                    e = jnp.exp2(steps[h, k] * r2)
                    q = e * v
                    v = q + drive[u, k] * wb[u][k]
                    t = e * s[u]
                    s[u] = t + v
                    kept_v[h, k, n] = q
                    kept_s[h, k, n] = t
                    products[n, pl.ds(cols * u + k, S, stride=K), :] = s[u] * grads[h, k]
                from_above[half, k, i] = v
        store_sums(g_read, jnp.maximum(at_pair - 1, 0), sums)

    def final_adjoint(i):
        at_pair = mid - 1 - i
        pair = (2 * at_pair, 2 * at_pair + 1)
        codes = two_rows(at_pair)
        set_drive(pair)
        through = [[jnp.zeros((S, D), F32)] * K for _ in range(2)]
        rated = [[jnp.zeros((S, D), F32)] * K for _ in range(2)]
        sums = jnp.zeros((NS, 2 * cols), F32)
        for n in range(NS):
            half, i = divmod(n, HALF)
            spreads = spread(codes, both, n)
            sums = sums + channel_sums(products[n], picker, n)
            r2 = rates[n]
            a = [jnp.exp2(-r2 * upto[h]) * later[h, half, pl.ds(i, S, stride=HALF), :]
                 for h in pair]
            stepped = jnp.zeros((S, D), F32)
            for k in reversed(range(K)):
                b = from_below[half, k, i]
                for u in (1, 0):
                    h = pair[u]
                    dt = steps[h, k]
                    e = jnp.exp2(dt * r2)
                    ah = a[u] + tile_of(spreads, cols * u + S * k, 1) * grads[h, k]
                    av = ah + b
                    b = e * av
                    a[u] = e * ah
                    eg = ah * kept_s[h, k, n] + av * kept_v[h, k, n]
                    through[u][k] = through[u][k] + av * tile_of(spreads, cols * u + S * k, 0)
                    rated[u][k] = rated[u][k] + eg * r2
                    stepped = stepped + eg * dt
                    products[n, pl.ds(cols * u + k, S, stride=K), :] = av * drive[u, k]
                from_below[half, k, i] = b
            part[n] += stepped
        store_sums(g_write, jnp.minimum(at_pair + 1, mid - 1), sums)
        for u, h in enumerate(pair):
            for k in range(K):
                g_feat[h, pl.ds(k, S, stride=K), :] = steps[h, k] * through[u][k]
                g_step[h, pl.ds(k, S, stride=K), :] = (
                    column(feat, h, k, K) * through[u][k] + LN2 * rated[u][k])

    def last_sums():
        sums = jnp.zeros((NS, 2 * cols), F32)
        for n in range(NS):
            sums = sums + channel_sums(products[n], picker, n)
        return sums

    def send(src, dst, sems, kind, o, peer):
        copy = pltpu.make_async_remote_copy(
            src_ref=src, dst_ref=dst, send_sem=sems.at[kind, o], recv_sem=sems.at[kind + 1, o],
            device_id=peer, device_id_type=MESH)
        copy.start()
        return copy

    def arrive(copies):
        for copy in copies:
            copy.wait()

    mine_k, mine_h = pl.ds(ri * kr, kr), pl.ds(ci * hc, hc)

    def scatter_rows(source, box, kind):
        box(ri)[...] = source(mine_k)[...]
        return [send(source(pl.ds(p[0] * kr, kr)), box(ri), row_sems, kind, o, p)
                for o, p in enumerate(row_peers)]

    def scatter_cols(source, box, kind):
        box(ci)[...] = source(mine_h)[...]
        return [send(source(pl.ds(p[1] * hc, hc)), box(ci), col_sems, kind, o, p)
                for o, p in enumerate(col_peers)]

    def return_rows(box, target, kind):
        target(mine_k)[...] = box(ri)[...]
        return [send(box(p[0]), target(mine_k), row_sems, kind, o, p)
                for o, p in enumerate(row_peers)]

    def return_cols(box, target, kind):
        target(mine_h)[...] = box[ci]
        return [send(box.at[p[1]], target(mine_h), col_sems, kind, o, p)
                for o, p in enumerate(col_peers)]

    def scan_cols(source, result, backward):
        for half in range(2):
            rate = slow[states_of(half), :]
            for j in range(hc):
                now = jnp.zeros((HALF, D), F32)
                for c in (reversed(range(nc)) if backward else range(nc)):
                    result[c, j, half] = now
                    now = jnp.exp2(rate * source[c, j, 2]) * now + source[c, j, half]

    fetches[0].wait()
    fetches[1].wait()
    lax.fori_loop(0, rows, code, 0, unroll=4)
    fetches[2].wait()
    fetches[3].wait()
    part_way = mid // 2

    def scan_rows(half, backward):
        def one(i, carry):
            r2 = rates[half * HALF + i]
            for j in range(kr):
                now = jnp.zeros((S, D), F32)
                for r in (reversed(range(nr)) if backward else range(nr)):
                    out_r[r, half, j, i] = now
                    now = jnp.exp2(r2 * in_r[r, 0, j, HALF]) * now + in_r[r, half, j, i]
            return carry

        lax.fori_loop(0, HALF, one, 0)

    def rows_out(half, leave, kind, width=HALF):
        part_of = pl.ds(0, width)
        return scatter_rows(lambda k: leave.at[half, k, part_of],
                            lambda r: in_r.at[r, half, :, part_of], kind)

    def rows_back(half, flight, backward, target, kind):
        arrive(flight)
        scan_rows(half, backward)
        return return_rows(lambda r: out_r.at[r, half], lambda k: target.at[half, k], kind)

    over(0, mid, functools.partial(local_vertical, 0))
    pl.semaphore_wait(barrier, len(row_peers) + len(col_peers))
    down = [None, None]
    down[0] = rows_out(0, leave_v, 0, HALF + 1)
    over(0, mid, functools.partial(local_vertical, 1))
    down[1] = rows_out(1, leave_v, 4)
    fetches[4].wait()
    over(0, mid, set_grads)
    over(0, part_way, local_adjoint)
    down[0] = rows_back(0, down[0], False, from_above, 2)
    over(part_way, mid, local_adjoint)
    right = scatter_cols(lambda h: leave_a.at[h], lambda c: in_c.at[c], 0)
    down[1] = rows_back(1, down[1], False, from_above, 6)
    arrive(down[0])
    leave_v[0, :, :HALF] = from_above[0]
    over(0, mid, functools.partial(carried_states, 0))
    arrive(right)
    scan_cols(in_c, out_c, True)
    right = return_cols(out_c, lambda h: from_right.at[h], 2)
    arrive(down[1])
    leave_v[1, :, :HALF] = from_above[1]
    over(0, mid, functools.partial(carried_states, 1))
    arrive(right)
    left = scatter_cols(lambda h: leave_s.at[h], lambda c: in_c.at[c, :, pl.ds(0, 2)], 6)
    over(0, mid, functools.partial(carried_adjoint, 0))
    up = [None, None]
    up[0] = rows_out(0, leave_p, 10)
    arrive(left)
    scan_cols(in_c, out_c, False)
    left = return_cols(out_c, lambda h: from_left.at[h], 8)
    over(0, mid, functools.partial(carried_adjoint, 1))
    up[1] = rows_out(1, leave_p, 14)
    arrive(left)
    over(0, part_way // 2, final_states)
    up[0] = rows_back(0, up[0], True, from_below, 12)
    over(part_way // 2, part_way, final_states)
    up[1] = rows_back(1, up[1], True, from_below, 16)
    over(part_way, mid, final_states)
    store_sums(g_read, mid - 1, last_sums())
    arrive(up[0])
    arrive(up[1])
    over(0, mid, final_adjoint)

    by_row[ri] = jnp.sum(part[...], axis=1)
    arrive([send(by_row.at[ri], by_row.at[ri], row_sems, 18, o, p)
            for o, p in enumerate(row_peers)])
    by_col[ci] = jnp.sum(by_row[...], axis=0)
    flight = [send(by_col.at[ci], by_col.at[ci], col_sems, 10, o, p)
              for o, p in enumerate(col_peers)]
    store_sums(g_write, 0, last_sums())
    arrive(flight)
    g_decay[...] = jnp.sum(by_col[...], axis=0) * -jnp.exp(decay_log[...])


def shards(features, step_size, write_weights, read_weights, decay_log, out_grad):
    rows, cols = step_size.shape[0], step_size.shape[1]
    K = cols // S
    nr, nc = lax.axis_size("row"), lax.axis_size("col")
    kr, hc = K // nr, rows // nc

    def vm(*shape, kind=F32):
        return pltpu.VMEM(shape, kind)

    carry_r, carry_c = vm(2, K, HALF, S, D), vm(rows, 2, HALF, D)
    grid, kept = vm(rows, K, S, D), vm(rows, K, NS, S, D)
    joined = vm(rows, 2, S * HALF, D)
    raw = vm(rows, cols, D)
    box_r = vm(nr, 2, kr, HALF, S, D)
    table = vm(6 * NS, NS * D, kind=BF16)
    box_c = vm(nc, hc, 2, HALF, D)
    args = (features, step_size, write_weights.transpose(0, 2, 1),
            read_weights.transpose(0, 2, 1), out_grad.reshape(NS, 2 * cols, D), decay_log)
    outs = [(rows, cols, D), (rows, cols, D), (rows, NS, cols), (rows, NS, cols), (NS, D)]
    g_feat, g_step, g_write, g_read, g_decay = pl.pallas_call(
        functools.partial(scan_kernel, nr, nc),
        out_shape=[jax.ShapeDtypeStruct(o, F32) for o in outs],
        in_specs=[pl.BlockSpec(memory_space=pl.ANY)] * 5 + [VMEM],
        out_specs=[VMEM] * len(outs),
        scratch_shapes=[
            vm(NS, S, D), vm(NS, D), table, table, vm(6 * NS, 2 * NS * D, kind=BF16),
            vm(NS, NS, 2 * D, kind=BF16), vm(rows * cols, 6 * NS, kind=BF16), grid, grid, vm(2, K, S, D),
            vm(rows, S, D), vm(rows, S, D), vm(rows, 1, D), joined, joined,
            vm(2, K, HALF + 1, S, D), carry_r, carry_r, carry_r,
            vm(rows, 3, HALF, D), carry_c, carry_c, carry_c, kept, kept,
            vm(NS, 2 * cols, D), vm(NS, S, D),
            vm(nr, 2, kr, HALF + 1, S, D), box_r, vm(nc, hc, 3, HALF, D), box_c, vm(nr, NS, D), vm(nc, NS, D),
            vm(rows, NS, cols), vm(rows, NS, cols), raw, raw,
            pltpu.SemaphoreType.DMA((20, nr - 1)), pltpu.SemaphoreType.DMA((12, nc - 1)),
            pltpu.SemaphoreType.DMA((5,))],
        compiler_params=pltpu.CompilerParams(
            collective_id=0, has_side_effects=True, vmem_limit_bytes=50 << 20),
        name="scan",
    )(*args)
    return (g_feat, g_step, g_write.transpose(0, 2, 1), g_read.transpose(0, 2, 1), g_decay)


def solution(mesh):
    tiles = P("row", "col", None)
    in_specs = (tiles, tiles, tiles, tiles, P(), tiles)
    out_specs = (tiles, tiles, tiles, tiles, P())
    return jax.shard_map(shards, mesh=mesh, in_specs=in_specs, out_specs=out_specs, check_vma=False)
```
